32 devices in a mesh: cells: 16 (over z, y, core), lanes: 2 (over x).
Axes of the slice: x: 2, y: 2, z: 4, core: 2. Of those that a mesh axis runs over, the one named last changes fastest.
Arguments:
- centres: float32 [3, 16384], P(None, 'cells'), may hold values from 0 to 4
- seg_lines: float32 [3, 16384], P(None, 'cells'), may hold values from -3 to 3
- burgers: float32 [3, 16384], P(None, 'cells'), may hold values from -6 to 6
- neighbour_blocks: int32 [128, 16], P('cells', 'lanes'), may hold values from 0 to 39
- seg_nodes: int32 [2, 16384], P(None, 'cells'), may hold values from 0 to 1023
- node_owner: int32 [2, 16384], P(None, 'cells'), may hold values from 0 to 1
- mobility: float32 [16384], P('cells'), may hold values from 0.5 to 4
- cand_target: int32 [512], P('cells'), may hold values from 0 to 7
- cand_source: int32 [512], P('cells'), may hold values from 0 to 39
Outputs:
- node_velocity: float32 [3, 16384], P(None, 'cells')
- nearness: float32 [16384], P('cells')
The draws below stay inside these ranges and needn't reach their ends.
All inputs are finite; a program needn't handle non-finite values.
Results may differ from the reference program's by a relative error of at most 0.0003.
Values sent between devices are 32-bit elements; how exact they have to be, the bound alone decides.
No kernel may reach another device: no remote copies, remote signals or barrier semaphores. Data moves between devices by JAX's collectives and lax.ppermute only.
A program may use at most 64 MiB of HBM per device.

```python
import math
import jax
import jax.numpy as jnp
from jax import lax

SEG = 1024
BLK = 128
NLIST = 16
NCAND = 32
REACH = 2
NB = 8
WIN = 40
SEGS = 16384
BLOCKS = 128
CANDS = 512
N_CELLS = 16


def set_ends(result, stream_key, least, high):
    extent = result.shape
    spot = [jax.random.randint(jax.random.fold_in(stream_key, axis), (), 0, extent[axis]) for axis in range(len(extent))]
    result = result.at[tuple(spot)].set(least)
    longest = extent.index(max(extent))
    spot[longest] = (spot[longest] + 1) % extent[longest]
    return result.at[tuple(spot)].set(high)


def level_of(own_key, dims, split, low, high):
    factor_of = 1.0
    for dim, parts in split:
        steps = jax.random.uniform(jax.random.fold_in(jax.random.fold_in(own_key, 6), dim), (parts,), jnp.float32, low / len(split), high / len(split))
        factor_of = factor_of * jnp.repeat(jnp.exp(steps), dims[dim] // parts).reshape((-1,) + (1,) * (len(dims) - 1 - dim))
    return factor_of


def scatter_about(key, shape, spread, bound, shards=(), kind=jnp.bfloat16):
    gain = level_of(key, shape, shards, -0.22, 0.18) if shards else 1.0
    result = jax.random.normal(key, shape, jnp.float32) * spread * gain
    return jnp.minimum(jnp.maximum(result, -bound), bound).astype(kind)


def setup_inputs(seed: int = 0) -> dict:
    arg_keys = jax.random.split(jax.random.key(seed), 10)
    return {
        "centres": jnp.clip(4.0 * jax.random.uniform(arg_keys[0], (3, SEGS), jnp.float32) ** level_of(arg_keys[0], (3, SEGS), ((1, 16),), -0.2, 0.2), 0.0, 4.0),
        "seg_lines": scatter_about(arg_keys[1], (3, SEGS), 0.5, 3.0, ((1, 16),), jnp.float32),
        "burgers": scatter_about(arg_keys[2], (3, SEGS), 1.0, 6.0, ((1, 16),), jnp.float32),
        "neighbour_blocks": set_ends(jax.random.randint(arg_keys[3], (BLOCKS, NLIST), 0, WIN), jax.random.fold_in(arg_keys[3], 1), 0, WIN - 1).astype(jnp.int32),
        "seg_nodes": set_ends(jax.random.randint(arg_keys[4], (2, SEGS), 0, SEG), jax.random.fold_in(arg_keys[4], 1), 0, SEG - 1).astype(jnp.int32),
        "node_owner": set_ends(jax.random.randint(arg_keys[5], (2, SEGS), 0, 2), jax.random.fold_in(arg_keys[5], 1), 0, 1).astype(jnp.int32),
        "mobility": jnp.clip(jnp.exp(math.log(4.0) - 2.0794415 * jax.random.uniform(arg_keys[6], (SEGS,), jnp.float32) ** level_of(arg_keys[6], (SEGS,), ((0, 16),), -0.2, 0.2)), 0.5, 4.0),
        "cand_target": set_ends(jax.random.randint(arg_keys[7], (CANDS,), 0, NB), jax.random.fold_in(arg_keys[7], 1), 0, NB - 1).astype(jnp.int32),
        "cand_source": set_ends(jax.random.randint(arg_keys[8], (CANDS,), 0, WIN), jax.random.fold_in(arg_keys[8], 1), 0, WIN - 1).astype(jnp.int32),
    }


FORCE_SCALE = 0.02
CORE_SQUARE = 0.25
TIME_STEP = 4.0
HIGH = lax.Precision.HIGHEST

def cross_product(first, second):
    return jnp.stack([first[1] * second[2] - first[2] * second[1], first[2] * second[0] - first[0] * second[2], first[0] * second[1] - first[1] * second[0]])

def tile_forces(own_blocks, source_blocks):
    target_centre = own_blocks[0:3]
    target_line = own_blocks[3:6]
    source_centre = source_blocks[0:3]
    source_line = source_blocks[3:6]
    source_burgers = source_blocks[6:9]
    along = jnp.einsum('ckj,cki->kij', source_burgers, target_line, precision=HIGH)
    separation = target_centre[:, :, :, None] - source_centre[:, :, None, :]
    square = lax.optimization_barrier(jnp.sum(separation * separation, axis=0)) + CORE_SQUARE
    inverse = lax.rsqrt(square)
    weight = along * inverse * inverse * inverse
    summed_line = jnp.einsum('kij,ckj->cki', weight, source_line, precision=HIGH)
    summed_moment = jnp.einsum('kij,ckj->cki', weight, cross_product(source_line, source_centre), precision=HIGH)
    return FORCE_SCALE * (cross_product(summed_line, target_centre) - summed_moment)

def block_forces(own_blocks, window_blocks, block_lists):

    def add_entry(summed, column):
        chosen = jnp.take(window_blocks, column, axis=1)
        return (summed + tile_forces(own_blocks, chosen), None)
    initial = jnp.zeros((3,) + own_blocks.shape[1:], jnp.float32)
    summed, unused = lax.scan(add_entry, initial, jnp.transpose(block_lists))
    return summed

def swept_tiles(own_blocks, window_blocks, targets, sources):
    target_side = jnp.take(own_blocks, targets, axis=1)
    source_side = jnp.take(window_blocks, sources, axis=1)
    separation = target_side[0:3, :, :, None] - source_side[0:3, :, None, :]
    motion = TIME_STEP * (target_side[3:6, :, :, None] - source_side[3:6, :, None, :])
    approach = lax.optimization_barrier(jnp.sum(separation * motion, axis=0))
    motion_square = lax.optimization_barrier(jnp.sum(motion * motion, axis=0))
    fraction = jnp.clip(-approach / (motion_square + CORE_SQUARE), 0.0, 1.0)
    closest = separation + fraction[None] * motion
    distance = lax.optimization_barrier(jnp.sum(closest * closest, axis=0))
    summed = lax.optimization_barrier(jnp.sum(jnp.exp(-distance), axis=2))
    selector = (targets[:, None] == jnp.arange(own_blocks.shape[1], dtype=jnp.int32)[None, :]).astype(jnp.float32)
    return jnp.einsum('nk,nb->kb', selector, summed, precision=HIGH)

def deposit(deposits, node_ids, keep_mask, node_count):
    masked = deposits * keep_mask.astype(jnp.float32)[None, :]
    return jnp.transpose(jax.ops.segment_sum(jnp.transpose(masked), node_ids, num_segments=node_count))

def end_velocity(velocity, next_velocity, node_ids, owner_map):
    return jnp.where(owner_map[None, :] == 0, jnp.take(velocity, node_ids, axis=1), jnp.take(next_velocity, node_ids, axis=1))

def window_of(fields, domain):
    picks = [lax.dynamic_index_in_dim(fields, (domain + offset) % N_CELLS, 1, keepdims=False) for offset in range(-REACH, REACH + 1)]
    return jnp.concatenate(picks, axis=1)

def reference(centres, seg_lines, burgers, neighbour_blocks, seg_nodes, node_owner, mobility, cand_target, cand_source):
    domains = jnp.arange(N_CELLS, dtype=jnp.int32)
    fields = jnp.concatenate([centres, seg_lines, burgers], 0).reshape(9, N_CELLS, SEG)
    block_lists = neighbour_blocks.reshape(N_CELLS, NB, NLIST)

    def forces_of(domain):
        own_blocks = lax.dynamic_index_in_dim(fields, domain, 1, keepdims=False).reshape(9, NB, BLK)
        window_blocks = window_of(fields, domain).reshape(9, WIN, BLK)
        chosen_lists = lax.dynamic_index_in_dim(block_lists, domain, 0, keepdims=False)
        return block_forces(own_blocks, window_blocks, chosen_lists).reshape(3, SEG)
    forces = lax.map(forces_of, domains)
    lengths = jnp.sqrt(lax.optimization_barrier(jnp.sum(seg_lines * seg_lines, axis=0))).reshape(N_CELLS, SEG)
    deposits = jnp.concatenate([0.5 * forces, 0.5 * lengths[:, None, :]], axis=1)
    node_ids = seg_nodes.reshape(2, N_CELLS, SEG)
    owner_map = node_owner.reshape(2, N_CELLS, SEG)

    def split_parts(domain_deposits, first_ids, second_ids, first_owner, second_owner):
        own_part = deposit(domain_deposits, first_ids, first_owner == 0, SEG) + deposit(domain_deposits, second_ids, second_owner == 0, SEG)
        next_part = deposit(domain_deposits, first_ids, first_owner == 1, SEG) + deposit(domain_deposits, second_ids, second_owner == 1, SEG)
        return (own_part, next_part)
    own_part, next_part = jax.vmap(split_parts)(deposits, node_ids[0], node_ids[1], owner_map[0], owner_map[1])
    totals = own_part + jnp.roll(next_part, 1, axis=0)
    velocity = mobility.reshape(N_CELLS, 1, SEG) * totals[:, 0:3] / (1.0 + totals[:, 3:4])
    next_velocity = jnp.roll(velocity, -1, axis=0)
    seg_velocity = 0.5 * (jax.vmap(end_velocity)(velocity, next_velocity, node_ids[0], owner_map[0]) + jax.vmap(end_velocity)(velocity, next_velocity, node_ids[1], owner_map[1]))
    motion_fields = jnp.concatenate([centres.reshape(3, N_CELLS, SEG), jnp.transpose(seg_velocity, (1, 0, 2))], axis=0)
    targets = cand_target.reshape(N_CELLS, NCAND)
    sources = cand_source.reshape(N_CELLS, NCAND)

    def nearness_of(domain):
        own_blocks = lax.dynamic_index_in_dim(motion_fields, domain, 1, keepdims=False).reshape(6, NB, BLK)
        window_blocks = window_of(motion_fields, domain).reshape(6, WIN, BLK)
        return swept_tiles(own_blocks, window_blocks, lax.dynamic_index_in_dim(targets, domain, 0, keepdims=False), lax.dynamic_index_in_dim(sources, domain, 0, keepdims=False)).reshape(SEG)
    nearness = lax.map(nearness_of, domains)
    return (jnp.transpose(velocity, (1, 0, 2)).reshape(3, N_CELLS * SEG), nearness.reshape(N_CELLS * SEG))
```

```python
import functools

import jax
import jax.numpy as jnp
from jax import lax
from jax.experimental import pallas as pl
from jax.experimental.pallas import tpu as pltpu
from jax.sharding import PartitionSpec as P

BLK = 128
REACH = 2
FORCE_SCALE = 0.02
CORE_SQUARE = 0.25
TIME_STEP = 4.0
MIDDLE = 2.0

F32 = jnp.float32
BF16 = jnp.bfloat16
VM = pl.BlockSpec(memory_space=pltpu.VMEM)
SM = pl.BlockSpec(memory_space=pltpu.SMEM)


def shifted(block, cell_step, lane_step):
    cells, lanes = lax.axis_size("cells"), lax.axis_size("lanes")
    route = []
    for c in range(cells):
        for l in range(lanes):
            source = ((c + cell_step) % cells) * lanes + (l + lane_step) % lanes
            route.append((source, c * lanes + l))
    return lax.ppermute(block, ("cells", "lanes"), route)


def split3(x):
    high = x.astype(BF16).astype(F32)
    rest = x - high
    mid = rest.astype(BF16).astype(F32)
    return high, mid, rest - mid


def cross_rows(a, b):
    return jnp.concatenate(
        [
            a[1:2] * b[2:3] - a[2:3] * b[1:2],
            a[2:3] * b[0:1] - a[0:1] * b[2:3],
            a[0:1] * b[1:2] - a[1:2] * b[0:1],
        ],
        0,
    )


def contract_lanes(a, b):
    return lax.dot_general(a, b, (((1,), (1,)), ((), ())), preferred_element_type=F32)


def end_address(pack, end, high_count):
    node = pack[9 + end : 10 + end].astype(jnp.int32)
    owner = pack[11 + end : 12 + end].astype(jnp.int32)
    return owner * high_count + node // BLK, node % BLK


def low_onehot(low):
    rows = lax.broadcasted_iota(jnp.int32, (BLK, low.shape[1]), 0)
    return (rows == low).astype(F32).astype(BF16)


def force_kernel(lanes, high_count, lists, *refs):
    packs = refs[: 2 * REACH + 1]
    own_out, next_out, rhs_s, src_s, lhs_s, force_s = refs[2 * REACH + 1 :]
    seg = packs[0].shape[1]
    blocks = seg // BLK
    one = jnp.ones((1, seg), F32)

    for d, ref in enumerate(packs):
        centre = ref[0:3] - MIDDLE
        line = ref[3:6]
        burgers = ref[6:9]
        square = jnp.sum(centre * centre, axis=0, keepdims=True)
        near = jnp.concatenate([-2.0 * centre, square, one, jnp.zeros((3, seg), F32)], 0)
        along = jnp.concatenate([jnp.zeros((5, seg), F32), burgers], 0)
        sums = jnp.concatenate(
            [line, cross_rows(line, centre), jnp.zeros((2, seg), F32)], 0
        )
        nh, nm, nl = split3(near)
        ah, am, al = split3(along)
        sh, sm, sl = split3(sums)
        near6 = jnp.concatenate([nh, nm, nh, nl, nh, nm], 0).astype(BF16)
        along6 = jnp.concatenate([ah, am, ah, al, ah, am], 0).astype(BF16)
        sums3 = jnp.concatenate([sh, sm, sl, jnp.zeros((8, seg), F32)], 0).astype(BF16)
        for k in range(blocks):
            cut = slice(k * BLK, (k + 1) * BLK)
            rhs_s[d * blocks + k, :, 0:BLK] = near6[:, cut]
            rhs_s[d * blocks + k, :, BLK : 2 * BLK] = along6[:, cut]
            src_s[d * blocks + k] = sums3[:, cut]
        if d == REACH:
            target = jnp.concatenate([centre, one, square + CORE_SQUARE, line], 0)
            th, tm, tl = split3(target)
            target6 = jnp.concatenate([th, th, tm, th, tl, tm], 0)
            for k in range(blocks):
                lhs_s[k] = target6[:, k * BLK : (k + 1) * BLK].T.astype(BF16)

    own = packs[REACH]

    def one_target(t, carry):
        lhs = lhs_s[t]
        total = jnp.zeros((32, BLK), F32)
        for e in range(lists.shape[1]):
            w = lists[t, e]
            both = jnp.dot(lhs, rhs_s[w], preferred_element_type=F32)
            inverse = lax.rsqrt(both[:, :BLK])
            weight = both[:, BLK:] * inverse * (inverse * inverse)
            high = weight.astype(BF16)
            low = (weight - high.astype(F32)).astype(BF16)
            src = src_s[w]
            total = total + contract_lanes(src, high) + contract_lanes(src, low)
        whole = total[0:8] + (total[8:16] + total[16:24])
        force_s[t] = whole
        return carry

    lax.fori_loop(0, blocks, one_target, 0)

    whole = jnp.concatenate([force_s[t] for t in range(blocks)], 1)
    centre = own[0:3] - MIDDLE
    line = own[3:6]
    force = (0.5 * FORCE_SCALE) * (cross_rows(whole[0:3], centre) - whole[3:6])
    length = jnp.sqrt(jnp.sum(line * line, axis=0, keepdims=True)) * (0.5 / lanes)
    parts = split3(jnp.concatenate([force, length], 0))
    rows16 = lax.broadcasted_iota(jnp.int32, (2 * high_count, seg), 0)
    pack = own[...]
    out = None
    for end in range(2):
        high, low = end_address(pack, end, high_count)
        mask = rows16 == high
        lhs = jnp.concatenate(
            [
                jnp.where(mask, part[k : k + 1], 0.0)
                for part in parts
                for k in range(4)
            ],
            0,
        ).astype(BF16)
        term = contract_lanes(lhs, low_onehot(low))
        out = term if out is None else out + term
    n = 8 * high_count
    out = out[0:n] + (out[n : 2 * n] + out[2 * n : 3 * n])
    for k in range(4):
        first = 2 * high_count * k
        own_out[k] = out[first : first + high_count]
        next_out[k] = out[first + high_count : first + 2 * high_count]


def near_kernel(high_count, targets, sources, *refs):
    packs = refs[: 2 * REACH + 1]
    velocities = refs[2 * REACH + 1 : 4 * REACH + 3]
    near_out, vel_out, tgt_s, src_s, acc_s = refs[4 * REACH + 3 :]
    seg = packs[0].shape[1]
    blocks = seg // BLK
    rows8 = lax.broadcasted_iota(jnp.int32, (high_count, seg), 0)

    for k in range(high_count):
        for x in range(3):
            vel_out[x : x + 1, k * BLK : (k + 1) * BLK] = velocities[REACH][x, k : k + 1, :]

    for d, ref in enumerate(packs):
        pack = ref[...]
        table = jnp.concatenate(
            [velocities[d][x] for x in range(3)] + [velocities[d + 1][x] for x in range(3)], 0
        )
        lhs = jnp.concatenate(split3(table), 0).astype(BF16)
        n = 6 * high_count
        picked = [None] * 3
        for end in range(2):
            high, low = end_address(pack, end, high_count)
            got = jnp.dot(lhs, low_onehot(low), preferred_element_type=F32)
            got = got[0:n] + (got[n : 2 * n] + got[2 * n : 3 * n])
            for owner in range(2):
                mask = rows8 + owner * high_count == high
                for x in range(3):
                    first = (3 * owner + x) * high_count
                    term = jnp.where(mask, got[first : first + high_count], 0.0)
                    picked[x] = term if picked[x] is None else picked[x] + term
        motion = jnp.concatenate(
            [jnp.sum(p, axis=0, keepdims=True) * (0.5 * TIME_STEP) for p in picked], 0
        )
        fields = jnp.concatenate([pack[0:3], motion, jnp.zeros((2, seg), F32)], 0)
        for k in range(blocks):
            src_s[d * blocks + k] = fields[:, k * BLK : (k + 1) * BLK]

    for t in range(blocks):
        columns = src_s[REACH * blocks + t].T
        for x in range(6):
            tgt_s[t, x] = jnp.broadcast_to(columns[:, x : x + 1], (BLK, BLK))
    acc_s[...] = jnp.zeros_like(acc_s)

    def one_pair(k, carry):
        t = targets[k]
        src = src_s[sources[k]]
        r = [tgt_s[t, x] - src[x : x + 1] for x in range(3)]
        v = [tgt_s[t, 3 + x] - src[3 + x : 4 + x] for x in range(3)]
        dot = r[0] * v[0] + r[1] * v[1] + r[2] * v[2]
        vv = v[0] * v[0] + v[1] * v[1] + v[2] * v[2] + CORE_SQUARE
        s = jnp.clip(-dot / vv, 0.0, 1.0)
        m = [r[x] + s * v[x] for x in range(3)]
        acc_s[t] += jnp.exp(-(m[0] * m[0] + m[1] * m[1] + m[2] * m[2]))
        return carry

    lax.fori_loop(0, targets.shape[0], one_pair, 0)

    ones = jnp.ones((8, BLK), BF16)
    for t in range(blocks):
        h, m, l = split3(acc_s[t])
        total = (
            contract_lanes(ones, h.astype(BF16))
            + contract_lanes(ones, m.astype(BF16))
            + contract_lanes(ones, l.astype(BF16))
        )
        near_out[t : t + 1] = total[0:1]


def local(
    centres, seg_lines, burgers, neighbour_blocks, seg_nodes, node_owner, mobility, cand_target, cand_source
):
    seg = centres.shape[1]
    blocks = seg // BLK
    high_count = mobility.shape[0] // BLK
    lanes = lax.axis_size("lanes")
    window = (2 * REACH + 1) * blocks
    own = jnp.concatenate(
        [centres, seg_lines, burgers, seg_nodes.astype(F32), node_owner.astype(F32)], 0
    )
    packs = [own if o == 0 else shifted(own, o, 0) for o in range(-REACH, REACH + 1)]
    part = jax.ShapeDtypeStruct((4, high_count, BLK), F32)
    own_part, next_part = pl.pallas_call(
        functools.partial(force_kernel, lanes, high_count),
        out_shape=(part, part),
        in_specs=[SM] + [VM] * len(packs),
        out_specs=(VM, VM),
        scratch_shapes=[
            pltpu.VMEM((window, 48, 2 * BLK), BF16),
            pltpu.VMEM((window, 32, BLK), BF16),
            pltpu.VMEM((blocks, BLK, 48), BF16),
            pltpu.VMEM((blocks, 8, BLK), F32),
        ],
        name="forces",
    )(neighbour_blocks, *packs)
    totals = own_part
    for lane in range(1, lanes):
        totals = totals + shifted(own_part, 0, lane)
    for lane in range(lanes):
        totals = totals + shifted(next_part, -1, lane)
    velocity = mobility.reshape(1, high_count, BLK) * totals[0:3] / (1.0 + totals[3:4])
    velocities = [
        velocity if o == 0 else shifted(velocity, o, 0) for o in range(-REACH, REACH + 2)
    ]
    near, vel = pl.pallas_call(
        functools.partial(near_kernel, high_count),
        out_shape=(
            jax.ShapeDtypeStruct((blocks, BLK), F32),
            jax.ShapeDtypeStruct((3, high_count * BLK), F32),
        ),
        in_specs=[SM, SM] + [VM] * (len(packs) + len(velocities)),
        out_specs=(VM, VM),
        scratch_shapes=[
            pltpu.VMEM((blocks, 6, BLK, BLK), F32),
            pltpu.VMEM((window, 8, BLK), F32),
            pltpu.VMEM((blocks, BLK, BLK), F32),
        ],
        name="nearness",
    )(cand_target, cand_source, *packs, *velocities)
    return vel, near.reshape(seg)


def solution(mesh):
    in_specs = (
        P(None, "cells"),
        P(None, "cells"),
        P(None, "cells"),
        P("cells", "lanes"),
        P(None, "cells"),
        P(None, "cells"),
        P("cells"),
        P("cells"),
        P("cells"),
    )
    out_specs = (P(None, "cells"), P("cells"))
    return jax.shard_map(local, mesh=mesh, in_specs=in_specs, out_specs=out_specs, check_vma=False)
```

```python
import functools

import jax
import jax.numpy as jnp
from jax import lax
from jax.experimental import pallas as pl
from jax.experimental.pallas import tpu as pltpu
from jax.sharding import PartitionSpec as P

BLK = 128
REACH = 2
FORCE_SCALE = 0.02
CORE_SQUARE = 0.25
TIME_STEP = 4.0
MIDDLE = 2.0

F32 = jnp.float32
BF16 = jnp.bfloat16
VM = pl.BlockSpec(memory_space=pltpu.VMEM)
SM = pl.BlockSpec(memory_space=pltpu.SMEM)


def params(mib):
    return pltpu.CompilerParams(vmem_limit_bytes=mib << 20)


def shifted(block, cell_step, lane_step):
    cells, lanes = lax.axis_size("cells"), lax.axis_size("lanes")
    route = []
    for c in range(cells):
        for l in range(lanes):
            source = ((c + cell_step) % cells) * lanes + (l + lane_step) % lanes
            route.append((source, c * lanes + l))
    return lax.ppermute(block, ("cells", "lanes"), route)


def split3(x):
    high = x.astype(BF16).astype(F32)
    rest = x - high
    mid = rest.astype(BF16).astype(F32)
    return high, mid, rest - mid


def cross_rows(a, b):
    return jnp.concatenate(
        [
            a[1:2] * b[2:3] - a[2:3] * b[1:2],
            a[2:3] * b[0:1] - a[0:1] * b[2:3],
            a[0:1] * b[1:2] - a[1:2] * b[0:1],
        ],
        0,
    )


def contract_lanes(a, b):
    return lax.dot_general(a, b, (((1,), (1,)), ((), ())), preferred_element_type=F32)


def end_address(pack, end, high_count):
    node = pack[9 + end : 10 + end].astype(jnp.int32)
    owner = pack[11 + end : 12 + end].astype(jnp.int32)
    return owner * high_count + node // BLK, node % BLK


def low_onehot(low):
    rows = lax.broadcasted_iota(jnp.int32, (BLK, low.shape[1]), 0)
    return (rows == low).astype(F32).astype(BF16)


def force_kernel(lanes, high_count, lists, *refs):
    packs = refs[: 2 * REACH + 1]
    own_out, next_out, rhs_s, src_s, lhs_s, force_s = refs[2 * REACH + 1 :]
    seg = packs[0].shape[1]
    blocks = seg // BLK
    one = jnp.ones((1, seg), F32)

    for d, ref in enumerate(packs):
        centre = ref[0:3] - MIDDLE
        line = ref[3:6]
        burgers = ref[6:9]
        square = jnp.sum(centre * centre, axis=0, keepdims=True)
        near = jnp.concatenate([-2.0 * centre, square, one, jnp.zeros((3, seg), F32)], 0)
        along = jnp.concatenate([jnp.zeros((5, seg), F32), burgers], 0)
        sums = jnp.concatenate(
            [line, cross_rows(line, centre), jnp.zeros((2, seg), F32)], 0
        )
        nh, nm, nl = split3(near)
        ah, am, al = split3(along)
        sh, sm, sl = split3(sums)
        near6 = jnp.concatenate([nh, nm, nh, nl, nh, nm], 0).astype(BF16)
        along6 = jnp.concatenate([ah, am, ah, al, ah, am], 0).astype(BF16)
        sums3 = jnp.concatenate([sh, sm, sl, jnp.zeros((8, seg), F32)], 0).astype(BF16)
        for k in range(blocks):
            cut = slice(k * BLK, (k + 1) * BLK)
            rhs_s[d * blocks + k, :, 0:BLK] = near6[:, cut]
            rhs_s[d * blocks + k, :, BLK : 2 * BLK] = along6[:, cut]
            src_s[d * blocks + k] = sums3[:, cut]
        if d == REACH:
            target = jnp.concatenate([centre, one, square + CORE_SQUARE, line], 0)
            th, tm, tl = split3(target)
            target6 = jnp.concatenate([th, th, tm, th, tl, tm], 0)
            for k in range(blocks):
                lhs_s[k] = target6[:, k * BLK : (k + 1) * BLK].T.astype(BF16)

    own = packs[REACH]

    def one_target(t, carry):
        lhs = lhs_s[t]
        highs, lows, srcs = [], [], []
        for e in range(lists.shape[1]):
            w = lists[t, e]
            both = jnp.dot(lhs, rhs_s[w], preferred_element_type=F32)
            inverse = lax.rsqrt(both[:, :BLK])
            weight = both[:, BLK:] * inverse * (inverse * inverse)
            high = weight.astype(BF16)
            highs.append(high)
            lows.append((weight - high.astype(F32)).astype(BF16))
            srcs.append(src_s[w])
        src = jnp.concatenate(srcs, 1)
        total = contract_lanes(jnp.concatenate(highs, 1), src)
        total = total + contract_lanes(jnp.concatenate(lows, 1), src)
        total = total.T
        force_s[t] = total[0:8] + (total[8:16] + total[16:24])
        return carry

    lax.fori_loop(0, blocks, one_target, 0)

    whole = jnp.concatenate([force_s[t] for t in range(blocks)], 1)
    centre = own[0:3] - MIDDLE
    line = own[3:6]
    force = (0.5 * FORCE_SCALE) * (cross_rows(whole[0:3], centre) - whole[3:6])
    length = jnp.sqrt(jnp.sum(line * line, axis=0, keepdims=True)) * (0.5 / lanes)
    parts = split3(jnp.concatenate([force, length], 0))
    rows16 = lax.broadcasted_iota(jnp.int32, (2 * high_count, seg), 0)
    pack = own[...]
    out = None
    for end in range(2):
        high, low = end_address(pack, end, high_count)
        mask = rows16 == high
        lhs = jnp.concatenate(
            [
                jnp.where(mask, part[k : k + 1], 0.0)
                for part in parts
                for k in range(4)
            ],
            0,
        ).astype(BF16)
        term = contract_lanes(lhs, low_onehot(low))
        out = term if out is None else out + term
    n = 8 * high_count
    out = out[0:n] + (out[n : 2 * n] + out[2 * n : 3 * n])
    for k in range(4):
        first = 2 * high_count * k
        own_out[k] = out[first : first + high_count]
        next_out[k] = out[first + high_count : first + 2 * high_count]


def near_kernel(high_count, targets, sources, *refs):
    packs = refs[: 2 * REACH + 1]
    velocities = refs[2 * REACH + 1 : 4 * REACH + 3]
    near_out, vel_out, tgt_s, src_s, acc_s = refs[4 * REACH + 3 :]
    seg = packs[0].shape[1]
    blocks = seg // BLK
    rows8 = lax.broadcasted_iota(jnp.int32, (high_count, seg), 0)

    for k in range(high_count):
        for x in range(3):
            vel_out[x : x + 1, k * BLK : (k + 1) * BLK] = velocities[REACH][x, k : k + 1, :]

    for d, ref in enumerate(packs):
        pack = ref[...]
        table = jnp.concatenate(
            [velocities[d][x] for x in range(3)] + [velocities[d + 1][x] for x in range(3)], 0
        )
        lhs = jnp.concatenate(split3(table), 0).astype(BF16)
        n = 6 * high_count
        picked = [None] * 3
        for end in range(2):
            high, low = end_address(pack, end, high_count)
            got = jnp.dot(lhs, low_onehot(low), preferred_element_type=F32)
            got = got[0:n] + (got[n : 2 * n] + got[2 * n : 3 * n])
            for owner in range(2):
                mask = rows8 + owner * high_count == high
                for x in range(3):
                    first = (3 * owner + x) * high_count
                    term = jnp.where(mask, got[first : first + high_count], 0.0)
                    picked[x] = term if picked[x] is None else picked[x] + term
        motion = jnp.concatenate(
            [jnp.sum(p, axis=0, keepdims=True) * (0.5 * TIME_STEP) for p in picked], 0
        )
        centre = pack[0:3] - MIDDLE
        cc = jnp.sum(centre * centre, axis=0, keepdims=True)
        vv = jnp.sum(motion * motion, axis=0, keepdims=True)
        cv = jnp.sum(centre * motion, axis=0, keepdims=True)
        one = jnp.ones((1, seg), F32)

        def zero(n):
            return jnp.zeros((n, seg), F32)

        columns = [
            [-2.0 * centre, cc, one, zero(11)],
            [-motion, cv, zero(1), -centre, zero(1), one, zero(6)],
            [zero(3), vv, zero(1), -2.0 * motion, one, zero(7)],
        ]
        for n, rows in enumerate(columns):
            h, m, l = split3(jnp.concatenate(rows, 0))
            six = jnp.concatenate([h, m, h, l, h, m], 0).astype(BF16)
            for k in range(blocks):
                src_s[d * blocks + k, :, n * BLK : (n + 1) * BLK] = six[:, k * BLK : (k + 1) * BLK]
        if d == REACH:
            h, m, l = split3(jnp.concatenate([centre, one, cc, motion, vv, cv, zero(6)], 0))
            six = jnp.concatenate([h, h, m, h, l, m], 0)
            for k in range(blocks):
                tgt_s[k] = six[:, k * BLK : (k + 1) * BLK].T.astype(BF16)

    acc_s[...] = jnp.zeros_like(acc_s)
    count = targets.shape[0]
    group = max(g for g in (1, 2, 4) if count % g == 0)

    def some_pairs(step, carry):
        for u in range(group):
            k = step * group + u
            t = targets[k]
            three = jnp.dot(tgt_s[t], src_s[sources[k]], preferred_element_type=F32)
            rr = three[:, 0:BLK]
            rv = three[:, BLK : 2 * BLK]
            vv = jnp.maximum(three[:, 2 * BLK : 3 * BLK], 0.0)
            s = jnp.clip(-rv / (vv + CORE_SQUARE), 0.0, 1.0)
            acc_s[t] += jnp.exp(-(rr + s * (2.0 * rv + s * vv)))
        return carry

    lax.fori_loop(0, count // group, some_pairs, 0)

    ones = jnp.ones((8, BLK), BF16)
    for t in range(blocks):
        total = acc_s[t]
        high = total.astype(BF16)
        low = (total - high.astype(F32)).astype(BF16)
        near_out[t : t + 1] = (contract_lanes(ones, high) + contract_lanes(ones, low))[0:1]


def velocity_kernel(mobility, *refs):
    out = refs[-1]
    total = refs[0][...]
    for ref in refs[1:-1]:
        total = total + ref[...]
    scale = mobility[...] / (1.0 + total[3])
    for x in range(3):
        out[x] = total[x] * scale


def local(
    centres, seg_lines, burgers, neighbour_blocks, seg_nodes, node_owner, mobility, cand_target, cand_source
):
    seg = centres.shape[1]
    blocks = seg // BLK
    high_count = mobility.shape[0] // BLK
    lanes = lax.axis_size("lanes")
    window = (2 * REACH + 1) * blocks
    pieces = [centres, seg_lines, burgers, seg_nodes.astype(F32), node_owner.astype(F32)]
    rows = sum(piece.shape[0] for piece in pieces)
    own, first = 0.0, 0
    for piece in pieces:
        last = first + piece.shape[0]
        own = own + jnp.pad(piece, ((first, rows - last), (0, 0)))
        first = last
    rate = mobility.reshape(high_count, BLK)
    packs = [own if o == 0 else shifted(own, o, 0) for o in range(-REACH, REACH + 1)]
    part = jax.ShapeDtypeStruct((4, high_count, BLK), F32)
    own_part, next_part = pl.pallas_call(
        functools.partial(force_kernel, lanes, high_count),
        out_shape=(part, part),
        in_specs=[SM] + [VM] * len(packs),
        out_specs=(VM, VM),
        scratch_shapes=[
            pltpu.VMEM((window, 48, 2 * BLK), BF16),
            pltpu.VMEM((window, 32, BLK), BF16),
            pltpu.VMEM((blocks, BLK, 48), BF16),
            pltpu.VMEM((blocks, 8, BLK), F32),
        ],
        compiler_params=params(16),
        name="forces",
    )(neighbour_blocks, *packs)
    terms = [own_part]
    terms += [shifted(own_part, 0, lane) for lane in range(1, lanes)]
    terms += [shifted(next_part, -1, lane) for lane in range(lanes)]
    velocity = pl.pallas_call(
        velocity_kernel,
        out_shape=jax.ShapeDtypeStruct((3, high_count, BLK), F32),
        in_specs=[VM] * (1 + len(terms)),
        out_specs=VM,
        compiler_params=params(4),
        name="velocity",
    )(rate, *terms)
    velocities = [
        velocity if o == 0 else shifted(velocity, o, 0) for o in range(-REACH, REACH + 2)
    ]
    near, vel = pl.pallas_call(
        functools.partial(near_kernel, high_count),
        out_shape=(
            jax.ShapeDtypeStruct((blocks, BLK), F32),
            jax.ShapeDtypeStruct((3, high_count * BLK), F32),
        ),
        in_specs=[SM, SM] + [VM] * (len(packs) + len(velocities)),
        out_specs=(VM, VM),
        scratch_shapes=[
            pltpu.VMEM((blocks, BLK, 96), BF16),
            pltpu.VMEM((window, 96, 3 * BLK), BF16),
            pltpu.VMEM((blocks, BLK, BLK), F32),
        ],
        compiler_params=params(16),
        name="nearness",
    )(cand_target, cand_source, *packs, *velocities)
    return vel, near.reshape(seg)


def solution(mesh):
    in_specs = (
        P(None, "cells"),
        P(None, "cells"),
        P(None, "cells"),
        P("cells", "lanes"),
        P(None, "cells"),
        P(None, "cells"),
        P("cells"),
        P("cells"),
        P("cells"),
    )
    out_specs = (P(None, "cells"), P("cells"))
    return jax.shard_map(local, mesh=mesh, in_specs=in_specs, out_specs=out_specs, check_vma=False)
```

```python
import functools
import math

import jax
import jax.numpy as jnp
from jax import lax
from jax.experimental import pallas as pl
from jax.experimental.pallas import tpu as pltpu
from jax.sharding import PartitionSpec as P

BLK = 128
REACH = 2
FORCE_SCALE = 0.02
CORE_SQUARE = 0.25
TIME_STEP = 4.0
MIDDLE = 2.0

F32 = jnp.float32
BF16 = jnp.bfloat16
VM = pl.BlockSpec(memory_space=pltpu.VMEM)
SM = pl.BlockSpec(memory_space=pltpu.SMEM)


def params(mib):
    return pltpu.CompilerParams(vmem_limit_bytes=mib << 20)


def shifted(block, cell_step, lane_step):
    cells, lanes = lax.axis_size("cells"), lax.axis_size("lanes")
    route = []
    for c in range(cells):
        for l in range(lanes):
            source = ((c + cell_step) % cells) * lanes + (l + lane_step) % lanes
            route.append((source, c * lanes + l))
    return lax.ppermute(block, ("cells", "lanes"), route)


def split3(x):
    high = x.astype(BF16).astype(F32)
    rest = x - high
    mid = rest.astype(BF16).astype(F32)
    return high, mid, rest - mid


def cross_rows(a, b):
    return jnp.concatenate(
        [
            a[1:2] * b[2:3] - a[2:3] * b[1:2],
            a[2:3] * b[0:1] - a[0:1] * b[2:3],
            a[0:1] * b[1:2] - a[1:2] * b[0:1],
        ],
        0,
    )


def contract_lanes(a, b):
    return lax.dot_general(a, b, (((1,), (1,)), ((), ())), preferred_element_type=F32)


def end_address(pack, end, high_count):
    node = pack[16 + end : 17 + end].astype(jnp.int32)
    owner = pack[18 + end : 19 + end].astype(jnp.int32)
    return owner * high_count + node // BLK, node % BLK


def six_left(x):
    h, m, l = split3(x)
    return jnp.concatenate([h, h, m, h, l, m], 0)


def six_right(x):
    h, m, l = split3(x)
    return jnp.concatenate([h, m, h, l, h, m], 0)


def pack_kernel(fields, out):
    seg = fields.shape[1]
    centre = fields[0:3] - MIDDLE
    line = fields[3:6]
    out[0:3] = -2.0 * centre
    out[3:4] = jnp.sum(centre * centre, axis=0, keepdims=True)
    out[4:5] = jnp.ones((1, seg), F32)
    out[5:8] = fields[6:9]
    out[8:11] = line
    out[11:14] = cross_rows(line, centre)
    out[14:16] = jnp.zeros((2, seg), F32)
    out[16:20] = fields[9:13]
    out[20:24] = jnp.zeros((4, seg), F32)


def low_onehot(low):
    rows = lax.broadcasted_iota(jnp.int32, (BLK, low.shape[1]), 0)
    return (rows == low).astype(F32).astype(BF16)


def early_kernel(high_count, own, *refs):
    count = (len(refs) - 2) // 2
    for source, out in zip(refs[:count], refs[count : 2 * count]):
        out[...] = source[...]
    lhs_out, onehots = refs[2 * count :]
    pack = own[...]
    target = jnp.concatenate(
        [-0.5 * pack[0:3], pack[4:5], pack[3:4] + CORE_SQUARE, pack[8:11]], 0
    )
    six = six_left(target)
    for k in range(own.shape[1] // BLK):
        lhs_out[k] = six[:, k * BLK : (k + 1) * BLK].T.astype(BF16)
    for end in range(2):
        onehots[end] = low_onehot(end_address(pack, end, high_count)[1])


def force_kernel(lanes, high_count, lists, lhs_s, onehots, *refs):
    packs = refs[: 2 * REACH + 1]
    own_out, next_out, rhs_s, src_s, force_s = refs[2 * REACH + 1 :]
    seg = packs[0].shape[1]
    blocks = seg // BLK
    rows = lax.broadcasted_iota(jnp.int32, (8, seg), 0)

    for d, ref in enumerate(packs):
        source = ref[0:8]
        h, m, l = split3(source)
        near = [jnp.where(rows < 5, x, 0.0) for x in (h, m, l)]
        along = [jnp.where(rows < 5, 0.0, x) for x in (h, m, l)]
        near6, along6 = [
            jnp.concatenate([x[0], x[1], x[0], x[2], x[0], x[1]], 0).astype(BF16)
            for x in (near, along)
        ]
        sums = split3(ref[8:16])
        sums3 = jnp.concatenate([*sums, jnp.zeros((8, seg), F32)], 0).astype(BF16)
        for k in range(blocks):
            cut = slice(k * BLK, (k + 1) * BLK)
            rhs_s[d * blocks + k, :, 0:BLK] = near6[:, cut]
            rhs_s[d * blocks + k, :, BLK : 2 * BLK] = along6[:, cut]
            src_s[d * blocks + k] = sums3[:, cut]
    own = packs[REACH]

    def one_target(t, carry):
        lhs = lhs_s[t]
        highs, lows, srcs = [], [], []
        for e in range(lists.shape[1]):
            w = lists[t, e]
            both = jnp.dot(lhs, rhs_s[w], preferred_element_type=F32)
            inverse = lax.rsqrt(both[:, :BLK])
            weight = both[:, BLK:] * inverse * (inverse * inverse)
            high = weight.astype(BF16)
            highs.append(high)
            lows.append((weight - high.astype(F32)).astype(BF16))
            srcs.append(src_s[w])
        src = jnp.concatenate(srcs, 1)
        total = contract_lanes(jnp.concatenate(highs, 1), src)
        total = total + contract_lanes(jnp.concatenate(lows, 1), src)
        total = total.T
        force_s[t] = total[0:8] + (total[8:16] + total[16:24])
        return carry

    lax.fori_loop(0, blocks, one_target, 0, unroll=math.gcd(blocks, 4))

    whole = jnp.concatenate([force_s[t] for t in range(blocks)], 1)
    centre = -0.5 * own[0:3]
    line = own[8:11]
    force = (0.5 * FORCE_SCALE) * (cross_rows(whole[0:3], centre) - whole[3:6])
    length = jnp.sqrt(jnp.sum(line * line, axis=0, keepdims=True)) * (0.5 / lanes)
    parts = split3(jnp.concatenate([force, length], 0))
    rows16 = lax.broadcasted_iota(jnp.int32, (2 * high_count, seg), 0)
    pack = own[...]
    out = None
    for end in range(2):
        mask = rows16 == end_address(pack, end, high_count)[0]
        lhs = jnp.concatenate(
            [
                jnp.where(mask, part[k : k + 1], 0.0)
                for part in parts
                for k in range(4)
            ],
            0,
        ).astype(BF16)
        term = contract_lanes(lhs, onehots[end])
        out = term if out is None else out + term
    n = 8 * high_count
    out = out[0:n] + (out[n : 2 * n] + out[2 * n : 3 * n])
    for k in range(4):
        first = 2 * high_count * k
        own_out[k] = out[first : first + high_count]
        next_out[k] = out[first + high_count : first + 2 * high_count]


def select_kernel(high_count, *refs):
    packs, (onehots, centre_out) = refs[:-2], refs[-2:]
    seg = packs[0].shape[1]
    blocks = seg // BLK
    rows = lax.broadcasted_iota(jnp.int32, (8, seg), 0)
    for d, ref in enumerate(packs):
        pack = ref[...]
        if d != REACH:
            slot = 2 * (d if d < REACH else d - 1)
            for end in range(2):
                onehots[slot + end] = low_onehot(end_address(pack, end, high_count)[1])
        near = six_right(jnp.where(rows < 5, pack[0:8], 0.0)).astype(BF16)
        for k in range(blocks):
            centre_out[d * blocks + k] = near[:, k * BLK : (k + 1) * BLK]


def near_kernel(high_count, targets, sources, own_onehots, onehots, centre_s, *refs):
    packs = refs[: 2 * REACH + 1]
    velocities = refs[2 * REACH + 1 : 4 * REACH + 3]
    near_out, vel_out, tgt_s, src_s, acc_s = refs[4 * REACH + 3 :]
    seg = packs[0].shape[1]
    blocks = seg // BLK
    rows8 = lax.broadcasted_iota(jnp.int32, (high_count, seg), 0)

    for k in range(high_count):
        for x in range(3):
            vel_out[x : x + 1, k * BLK : (k + 1) * BLK] = velocities[REACH][x, k : k + 1, :]

    one = jnp.ones((1, seg), F32)

    def zero(n):
        return jnp.zeros((n, seg), F32)

    for d, ref in enumerate(packs):
        pack = ref[...]
        table = jnp.concatenate(
            [velocities[d][x] for x in range(3)] + [velocities[d + 1][x] for x in range(3)], 0
        )
        top = table.astype(BF16).astype(F32)
        lhs = jnp.concatenate([top, table - top], 0).astype(BF16)
        n = 6 * high_count
        picked = [None] * 3
        for end in range(2):
            high = end_address(pack, end, high_count)[0]
            slot = 2 * (d if d < REACH else d - 1) + end
            onehot = own_onehots[end] if d == REACH else onehots[slot]
            got = jnp.dot(lhs, onehot, preferred_element_type=F32)
            got = got[0:n] + got[n : 2 * n]
            for owner in range(2):
                mask = rows8 + owner * high_count == high
                for x in range(3):
                    first = (3 * owner + x) * high_count
                    term = jnp.where(mask, got[first : first + high_count], 0.0)
                    picked[x] = term if picked[x] is None else picked[x] + term
        motion = jnp.concatenate(
            [jnp.sum(p, axis=0, keepdims=True) * (0.5 * TIME_STEP) for p in picked], 0
        )
        centre = -0.5 * pack[0:3]
        vv = jnp.sum(motion * motion, axis=0, keepdims=True)
        cv = jnp.sum(centre * motion, axis=0, keepdims=True)
        columns = [
            [[-motion, cv, zero(4)], [-centre, zero(1), one, zero(3)]],
            [[zero(3), vv, zero(4)], [-2.0 * motion, one, zero(4)]],
        ]
        for n, pair in enumerate(columns):
            six = jnp.concatenate(
                [six_right(jnp.concatenate(rows, 0)) for rows in pair], 0
            ).astype(BF16)
            for k in range(blocks):
                src_s[d * blocks + k, :, n * BLK : (n + 1) * BLK] = six[:, k * BLK : (k + 1) * BLK]
        if d == REACH:
            six = jnp.concatenate(
                [
                    six_left(jnp.concatenate([centre, one, pack[3:4], zero(3)], 0)),
                    six_left(jnp.concatenate([motion, vv, cv, zero(3)], 0)),
                ],
                0,
            )
            for k in range(blocks):
                tgt_s[k] = six[:, k * BLK : (k + 1) * BLK].T.astype(BF16)

    acc_s[...] = jnp.zeros_like(acc_s)
    count = targets.shape[1]
    group = max(g for g in (1, 2, 4, 8, 16) if count % g == 0)

    def some_pairs(step, carry):
        for u in range(group):
            k = step * group + u
            t = targets[0, k]
            w = sources[0, k]
            target = tgt_s[t]
            rr = jnp.dot(target[:, 0:48], centre_s[w], preferred_element_type=F32)
            both = jnp.dot(target, src_s[w], preferred_element_type=F32)
            rv = both[:, 0:BLK]
            vv = jnp.maximum(both[:, BLK : 2 * BLK], 0.0)
            s = jnp.clip(-rv / (vv + CORE_SQUARE), 0.0, 1.0)
            acc_s[t] += jnp.exp(-(rr + s * (2.0 * rv + s * vv)))
        return carry

    lax.fori_loop(0, count // group, some_pairs, 0)

    ones = jnp.ones((8, BLK), BF16)
    for t in range(blocks):
        total = acc_s[t]
        high = total.astype(BF16)
        low = (total - high.astype(F32)).astype(BF16)
        near_out[t : t + 1] = (contract_lanes(ones, high) + contract_lanes(ones, low))[0:1]


def velocity_kernel(mobility, *refs):
    out = refs[-1]
    total = refs[0][...]
    for ref in refs[1:-1]:
        total = total + ref[...]
    scale = mobility[...] / (1.0 + total[3])
    for x in range(3):
        out[x] = total[x] * scale


def rows_of(pieces, first, rows):
    total = None
    for piece in pieces:
        last = first + piece.shape[0]
        padded = jnp.pad(piece, ((first, rows - last), (0, 0)))
        total = padded if total is None else total + padded
        first = last
    return total


def local(
    centres, seg_lines, burgers, neighbour_blocks, seg_nodes, node_owner, mobility, cand_target, cand_source
):
    seg = centres.shape[1]
    blocks = seg // BLK
    high_count = mobility.shape[0] // BLK
    lanes = lax.axis_size("lanes")
    window = (2 * REACH + 1) * blocks
    fields = rows_of([centres, seg_lines, burgers], 0, 13)
    fields = fields + rows_of([seg_nodes, node_owner], 9, 13).astype(F32)
    own = pl.pallas_call(
        pack_kernel,
        out_shape=jax.ShapeDtypeStruct((24, seg), F32),
        in_specs=[VM],
        out_specs=VM,
        compiler_params=params(4),
        name="pack",
    )(fields)
    packs = [own if o == 0 else shifted(own, o, 0) for o in range(-REACH, REACH + 1)]
    small = [
        neighbour_blocks,
        mobility.reshape(high_count, BLK),
        cand_target.reshape(1, -1),
        cand_source.reshape(1, -1),
    ]
    lists, rate, targets, sources, lhs, own_onehots = pl.pallas_call(
        functools.partial(early_kernel, high_count),
        out_shape=[jax.ShapeDtypeStruct(x.shape, x.dtype) for x in small]
        + [
            jax.ShapeDtypeStruct((blocks, BLK, 48), BF16),
            jax.ShapeDtypeStruct((2, BLK, seg), BF16),
        ],
        in_specs=[VM] * (1 + len(small)),
        out_specs=[VM] * (2 + len(small)),
        compiler_params=params(8),
        cost_estimate=pl.CostEstimate(flops=1 << 28, bytes_accessed=1 << 23, transcendentals=0),
        name="early",
    )(own, *small)
    part = jax.ShapeDtypeStruct((4, high_count, BLK), F32)
    own_part, next_part = pl.pallas_call(
        functools.partial(force_kernel, lanes, high_count),
        out_shape=(part, part),
        in_specs=[SM] + [VM] * (2 + len(packs)),
        out_specs=(VM, VM),
        scratch_shapes=[
            pltpu.VMEM((window, 48, 2 * BLK), BF16),
            pltpu.VMEM((window, 32, BLK), BF16),
            pltpu.VMEM((blocks, 8, BLK), F32),
        ],
        compiler_params=params(16),
        name="forces",
    )(lists, lhs, own_onehots, *packs)
    terms = [own_part]
    terms += [shifted(own_part, 0, lane) for lane in range(1, lanes)]
    terms += [shifted(next_part, -1, lane) for lane in range(lanes)]
    velocity = pl.pallas_call(
        velocity_kernel,
        out_shape=jax.ShapeDtypeStruct((3, high_count, BLK), F32),
        in_specs=[VM] * (1 + len(terms)),
        out_specs=VM,
        compiler_params=params(4),
        name="velocity",
    )(rate, *terms)
    velocities = [
        velocity if o == 0 else shifted(velocity, o, 0) for o in range(-REACH, REACH + 2)
    ]
    onehots, near_sources = pl.pallas_call(
        functools.partial(select_kernel, high_count),
        out_shape=(
            jax.ShapeDtypeStruct((2 * len(packs) - 2, BLK, seg), BF16),
            jax.ShapeDtypeStruct((window, 48, BLK), BF16),
        ),
        in_specs=[VM] * len(packs),
        out_specs=(VM, VM),
        compiler_params=params(16),
        cost_estimate=pl.CostEstimate(flops=1 << 28, bytes_accessed=1 << 23, transcendentals=0),
        name="select",
    )(*packs)
    near, vel = pl.pallas_call(
        functools.partial(near_kernel, high_count),
        out_shape=(
            jax.ShapeDtypeStruct((blocks, BLK), F32),
            jax.ShapeDtypeStruct((3, high_count * BLK), F32),
        ),
        in_specs=[SM, SM] + [VM] * (3 + len(packs) + len(velocities)),
        out_specs=(VM, VM),
        scratch_shapes=[
            pltpu.VMEM((blocks, BLK, 96), BF16),
            pltpu.VMEM((window, 96, 2 * BLK), BF16),
            pltpu.VMEM((blocks, BLK, BLK), F32),
        ],
        compiler_params=params(16),
        name="nearness",
    )(targets, sources, own_onehots, onehots, near_sources, *packs, *velocities)
    return vel, near.reshape(seg)


def solution(mesh):
    in_specs = (
        P(None, "cells"),
        P(None, "cells"),
        P(None, "cells"),
        P("cells", "lanes"),
        P(None, "cells"),
        P(None, "cells"),
        P("cells"),
        P("cells"),
        P("cells"),
    )
    out_specs = (P(None, "cells"), P("cells"))
    return jax.shard_map(local, mesh=mesh, in_specs=in_specs, out_specs=out_specs, check_vma=False)
```

```python
import functools
import math

import jax
import jax.numpy as jnp
from jax import lax
from jax.experimental import pallas as pl
from jax.experimental.pallas import tpu as pltpu
from jax.sharding import PartitionSpec as P

BLK = 128
FIELDS = 13
REACH = 2
FORCE_SCALE = 0.02
CORE_SQUARE = 0.25
TIME_STEP = 4.0
MIDDLE = 2.0
LOG2E = math.log2(math.e)

F32 = jnp.float32
BF16 = jnp.bfloat16
VM = pl.BlockSpec(memory_space=pltpu.VMEM)
SM = pl.BlockSpec(memory_space=pltpu.SMEM)


def params(mib):
    return pltpu.CompilerParams(vmem_limit_bytes=mib << 20)


def shifted(block, cell_step, lane_step):
    cells, lanes = lax.axis_size("cells"), lax.axis_size("lanes")
    route = []
    for c in range(cells):
        for l in range(lanes):
            source = ((c + cell_step) % cells) * lanes + (l + lane_step) % lanes
            route.append((source, c * lanes + l))
    return lax.ppermute(block, ("cells", "lanes"), route)


def split3(x):
    high = x.astype(BF16).astype(F32)
    rest = x - high
    mid = rest.astype(BF16).astype(F32)
    return high, mid, rest - mid


def row(ref, field, k):
    blocks = ref.shape[0] // FIELDS
    return ref[pl.ds(field * blocks + k, 8, stride=0), :]


def rows_at(ref, field, k):
    blocks = ref.shape[0] // FIELDS
    return ref[pl.ds(field * blocks + k, 8, stride=blocks), :]


def cross(a, b):
    return [
        a[1] * b[2] - a[2] * b[1],
        a[2] * b[0] - a[0] * b[2],
        a[0] * b[1] - a[1] * b[0],
    ]


def dot3(a, b):
    return a[0] * b[0] + a[1] * b[1] + a[2] * b[2]


def choose(rows, values, other):
    for number, value in values.items():
        other = jnp.where(rows == number, value, other)
    return other


def contract_lanes(a, b):
    return lax.dot_general(a, b, (((1,), (1,)), ((), ())), preferred_element_type=F32)


def end_address(ref, end, k, high_count):
    node = row(ref, 9 + end, k).astype(jnp.int32)
    owner = row(ref, 11 + end, k).astype(jnp.int32)
    return owner * high_count + lax.shift_right_logical(node, BLK.bit_length() - 1), node & (BLK - 1)


def six_left(x):
    h, m, l = split3(x)
    return jnp.concatenate([h, h, m, h, l, m], 0)


def right_order(parts):
    h, m, l = parts
    return jnp.concatenate([h, m, h, l, h, m], 0).astype(BF16)


def pack_kernel(fields, out):
    blocks = fields.shape[1] // BLK
    for k in range(blocks):
        piece = fields[:, k * BLK : (k + 1) * BLK]
        rows = lax.broadcasted_iota(jnp.int32, piece.shape, 0)
        out[pl.ds(k, FIELDS, stride=blocks), :] = jnp.where(rows < 3, piece - MIDDLE, piece)


def early_kernel(high_count, own, *refs):
    count = (len(refs) - 2) // 2
    for source, out in zip(refs[:count], refs[count : 2 * count]):
        out[...] = source[...]
    lhs_out, onehots = refs[2 * count :]
    rows = lax.broadcasted_iota(jnp.int32, (8, BLK), 0)
    nodes = lax.broadcasted_iota(jnp.int32, (BLK, BLK), 0)
    for k in range(own.shape[0] // FIELDS):
        c = [row(own, x, k) for x in range(3)]
        l = {3 + x: row(own, 6 + x, k) for x in range(3)}
        target = choose(rows, {**l, 6: 1.0, 7: dot3(c, c) + CORE_SQUARE}, rows_at(own, 0, k))
        lhs_out[k] = six_left(target).T.astype(BF16)
        for end in range(2):
            low = end_address(own, end, k, high_count)[1]
            onehots[end, :, k * BLK : (k + 1) * BLK] = (nodes == low[0:1]).astype(F32).astype(BF16)


def force_kernel(lanes, high_count, lists, lhs_s, onehots, *refs):
    packs = refs[: 2 * REACH + 1]
    own_out, next_out, rhs_s, src_s, force_s = refs[2 * REACH + 1 :]
    own = packs[REACH]
    blocks = own.shape[0] // FIELDS
    rows = lax.broadcasted_iota(jnp.int32, (8, BLK), 0)

    for d, ref in enumerate(packs):
        for k in range(blocks):
            c = [row(ref, x, k) for x in range(3)]
            l = [row(ref, 6 + x, k) for x in range(3)]
            upper, lower = rows_at(ref, 0, k), rows_at(ref, 5, k)
            near = jnp.where(rows < 3, -2.0 * upper, choose(rows, {6: dot3(c, c), 7: 1.0}, 0.0))
            along = jnp.where((rows >= 3) & (rows < 6), upper, 0.0)
            moment = cross(l, c)
            sums = choose(rows, {5 + x: moment[x] for x in range(3)}, lower)
            w = d * blocks + k
            rhs_s[w, :, 0:BLK] = right_order(split3(near))
            rhs_s[w, :, BLK : 2 * BLK] = right_order(split3(along))
            src_s[w] = jnp.concatenate([*split3(sums), jnp.zeros((8, BLK), F32)], 0).astype(BF16)

    def one_target(t, carry):
        lhs = lhs_s[t]
        highs, lows, srcs = [], [], []
        for e in range(lists.shape[1]):
            w = lists[t, e]
            both = jnp.dot(lhs, rhs_s[w], preferred_element_type=F32)
            inverse = lax.rsqrt(both[:, :BLK])
            weight = both[:, BLK:] * inverse * (inverse * inverse)
            high = weight.astype(BF16)
            highs.append(high)
            lows.append((weight - high.astype(F32)).astype(BF16))
            srcs.append(src_s[w])
        src = jnp.concatenate(srcs, 1)
        total = contract_lanes(jnp.concatenate(highs, 1), src)
        total = total + contract_lanes(jnp.concatenate(lows, 1), src)
        total = total.T
        force_s[t] = total[0:8] + (total[8:16] + total[16:24])
        return carry

    lax.fori_loop(0, blocks, one_target, 0, unroll=math.gcd(blocks, 4))

    out = None
    for k in range(blocks):
        whole = force_s.at[k]
        line = [whole[pl.ds(1 + x, 8, stride=0), :] for x in range(3)]
        moment = [whole[pl.ds(5 + x, 8, stride=0), :] for x in range(3)]
        c = [row(own, x, k) for x in range(3)]
        l = [row(own, 6 + x, k) for x in range(3)]
        turned = cross(line, c)
        values = [(0.5 * FORCE_SCALE) * (turned[x] - moment[x]) for x in range(3)]
        values.append(jnp.sqrt(dot3(l, l)) * (0.5 / lanes))
        tops = [value.astype(BF16).astype(F32) for value in values]
        parts = tops + [value - top for value, top in zip(values, tops)]
        pieces = []
        for end in range(2):
            high = end_address(own, end, k, high_count)[0]
            groups = range(0, 2 * high_count, 8)
            masks = [rows + first == high for first in groups]
            pieces.append([jnp.where(mask, part, 0.0) for part in parts for mask in masks])
        lhs = jnp.concatenate([jnp.concatenate(p, 0) for p in pieces], 1).astype(BF16)
        cut = slice(k * BLK, (k + 1) * BLK)
        term = contract_lanes(lhs, jnp.concatenate([onehots[end, :, cut] for end in range(2)], 1))
        out = term if out is None else out + term
    n = 8 * high_count
    out = out[0:n] + out[n : 2 * n]
    for k in range(4):
        first = 2 * high_count * k
        own_out[k] = out[first : first + high_count]
        next_out[k] = out[first + high_count : first + 2 * high_count]


def select_kernel(*refs):
    packs, (near_out, centre_out) = refs[:-2], refs[-2:]
    blocks = packs[0].shape[0] // FIELDS
    rows = lax.broadcasted_iota(jnp.int32, (8, BLK), 0)
    for d, ref in enumerate(packs):
        for k in range(blocks):
            w = d * blocks + k
            c = [row(ref, x, k) for x in range(3)]
            centre = LOG2E * rows_at(ref, 0, k)
            extra = choose(rows, {6: LOG2E * dot3(c, c), 7: LOG2E}, 0.0)
            near_out[w] = right_order(split3(jnp.where(rows < 3, -2.0 * centre, extra)))
            parts = split3(jnp.where(rows < 3, centre, choose(rows, {6: -LOG2E}, 0.0)))
            centre_out[w] = jnp.concatenate(parts, 0)


def near_kernel(high_count, targets, sources, near_s, centre_s, *refs):
    packs = refs[: 2 * REACH + 1]
    velocities = refs[2 * REACH + 1 : 4 * REACH + 3]
    near_out, vel_out, tgt_s, src_s, acc_s = refs[4 * REACH + 3 :]
    blocks = packs[0].shape[0] // FIELDS
    rows = lax.broadcasted_iota(jnp.int32, (8, BLK), 0)

    for k in range(high_count):
        for x in range(3):
            vel_out[x : x + 1, k * BLK : (k + 1) * BLK] = velocities[REACH][x, k : k + 1, :]

    zero = jnp.zeros((8, BLK), F32)
    nothing = jnp.zeros((48, BLK), BF16)
    signs = choose(rows, {4: -LOG2E}, zero + LOG2E)
    turn = jnp.where(rows < 3, -2.0, choose(rows, {3: 1.0}, zero))
    constant = split3(choose(rows, {5: LOG2E}, zero))
    for d, ref in enumerate(packs):
        for k in range(blocks):
            w = d * blocks + k
            v = [zero] * 3
            for end in range(2):
                high, low = end_address(ref, end, k, high_count)
                for owner in range(2):
                    for first in range(0, high_count, 8):
                        mask = rows + (owner * high_count + first) == high
                        for x in range(3):
                            table = velocities[d + owner][x, first : first + 8, :]
                            got = jnp.take_along_axis(table, low, axis=1, mode="promise_in_bounds")
                            v[x] = v[x] + jnp.where(mask, got, 0.0)
            for x in range(3):
                for shift in (4, 2, 1):
                    v[x] = v[x] + pltpu.roll(v[x], shift, 0)
                v[x] = v[x] * (0.5 * TIME_STEP)
            c = [row(ref, x, k) for x in range(3)]
            vv, cv = dot3(v, v), dot3(c, v)
            moved = choose(rows, {0: v[0], 1: v[1], 2: v[2], 3: vv}, cv)
            parts = split3(moved * signs)
            centre = centre_s[w]
            still = [centre[8 * n : 8 * n + 8] for n in range(3)]
            src_s[w, 0:48, 0:BLK] = right_order([jnp.where(rows < 3, p, 0.0) for p in parts])
            src_s[w, 48:96, 0:BLK] = right_order(
                [jnp.where(rows == 4, p, q) for p, q in zip(parts, still)]
            )
            src_s[w, 0:48, BLK : 2 * BLK] = nothing
            src_s[w, 48:96, BLK : 2 * BLK] = right_order(
                [p * turn + q for p, q in zip(parts, constant)]
            )
            if d == REACH:
                first = choose(rows, {6: 1.0, 7: dot3(c, c)}, rows_at(ref, 0, k))
                second = choose(rows, {3: 1.0, 4: 1.0, 5: vv, 6: cv, 7: 0.0}, moved)
                six = jnp.concatenate([six_left(first), six_left(second)], 0)
                tgt_s[k] = six.T.astype(BF16)

    acc_s[...] = jnp.zeros_like(acc_s)
    count = targets.shape[1]
    group = math.gcd(count, 16)

    def some_pairs(step, carry):
        for u in range(group):
            t = targets[0, step * group + u]
            w = sources[0, step * group + u]
            target = tgt_s[t]
            rr = jnp.dot(target[:, 0:48], near_s[w], preferred_element_type=F32)
            both = jnp.dot(target, src_s[w], preferred_element_type=F32)
            toward = both[:, 0:BLK]
            square = jnp.maximum(both[:, BLK : 2 * BLK], 0.0)
            s = jnp.clip(toward / (square + LOG2E * CORE_SQUARE), 0.0, 1.0)
            acc_s[t] += jnp.exp2(s * (toward + (toward - s * square)) - rr)
        return carry

    lax.fori_loop(0, count // group, some_pairs, 0)
    for t in range(blocks):
        near_out[t : t + 1] = jnp.sum(acc_s[t].T, axis=0, keepdims=True)


def velocity_kernel(mobility, *refs):
    out = refs[-1]
    total = refs[0][...]
    for ref in refs[1:-1]:
        total = total + ref[...]
    scale = mobility[...] / (1.0 + total[3])
    for x in range(3):
        out[x] = total[x] * scale


def rows_of(pieces, first, rows):
    total = None
    for piece in pieces:
        last = first + piece.shape[0]
        padded = jnp.pad(piece, ((first, rows - last), (0, 0)))
        total = padded if total is None else total + padded
        first = last
    return total


def local(
    centres, seg_lines, burgers, neighbour_blocks, seg_nodes, node_owner, mobility, cand_target, cand_source
):
    seg = centres.shape[1]
    blocks = seg // BLK
    high_count = mobility.shape[0] // BLK
    lanes = lax.axis_size("lanes")
    window = (2 * REACH + 1) * blocks
    fields = rows_of([centres, burgers, seg_lines], 0, FIELDS)
    fields = fields + rows_of([seg_nodes, node_owner], 9, FIELDS).astype(F32)
    own = pl.pallas_call(
        pack_kernel,
        out_shape=jax.ShapeDtypeStruct((FIELDS * blocks, BLK), F32),
        in_specs=[VM],
        out_specs=VM,
        compiler_params=params(4),
        name="pack",
    )(fields)
    packs = [own if o == 0 else shifted(own, o, 0) for o in range(-REACH, REACH + 1)]
    small = [
        neighbour_blocks,
        mobility.reshape(high_count, BLK),
        cand_target.reshape(1, -1),
        cand_source.reshape(1, -1),
    ]
    lists, rate, targets, sources, lhs, own_onehots = pl.pallas_call(
        functools.partial(early_kernel, high_count),
        out_shape=[jax.ShapeDtypeStruct(x.shape, x.dtype) for x in small]
        + [
            jax.ShapeDtypeStruct((blocks, BLK, 48), BF16),
            jax.ShapeDtypeStruct((2, BLK, seg), BF16),
        ],
        in_specs=[VM] * (1 + len(small)),
        out_specs=[VM] * (2 + len(small)),
        compiler_params=params(8),
        cost_estimate=pl.CostEstimate(flops=1 << 28, bytes_accessed=1 << 23, transcendentals=0),
        name="early",
    )(own, *small)
    part = jax.ShapeDtypeStruct((4, high_count, BLK), F32)
    own_part, next_part = pl.pallas_call(
        functools.partial(force_kernel, lanes, high_count),
        out_shape=(part, part),
        in_specs=[SM] + [VM] * (2 + len(packs)),
        out_specs=(VM, VM),
        scratch_shapes=[
            pltpu.VMEM((window, 48, 2 * BLK), BF16),
            pltpu.VMEM((window, 32, BLK), BF16),
            pltpu.VMEM((blocks, 8, BLK), F32),
        ],
        compiler_params=params(16),
        name="forces",
    )(lists, lhs, own_onehots, *packs)
    terms = [own_part]
    terms += [shifted(own_part, 0, lane) for lane in range(1, lanes)]
    terms += [shifted(next_part, -1, lane) for lane in range(lanes)]
    velocity = pl.pallas_call(
        velocity_kernel,
        out_shape=jax.ShapeDtypeStruct((3, high_count, BLK), F32),
        in_specs=[VM] * (1 + len(terms)),
        out_specs=VM,
        compiler_params=params(4),
        name="velocity",
    )(rate, *terms)
    velocities = [
        velocity if o == 0 else shifted(velocity, o, 0) for o in range(-REACH, REACH + 2)
    ]
    near_sources, centre_sources = pl.pallas_call(
        select_kernel,
        out_shape=(
            jax.ShapeDtypeStruct((window, 48, BLK), BF16),
            jax.ShapeDtypeStruct((window, 24, BLK), F32),
        ),
        in_specs=[VM] * len(packs),
        out_specs=(VM, VM),
        compiler_params=params(16),
        cost_estimate=pl.CostEstimate(flops=1 << 28, bytes_accessed=1 << 23, transcendentals=0),
        name="select",
    )(*packs)
    near, vel = pl.pallas_call(
        functools.partial(near_kernel, high_count),
        out_shape=(
            jax.ShapeDtypeStruct((blocks, BLK), F32),
            jax.ShapeDtypeStruct((3, high_count * BLK), F32),
        ),
        in_specs=[SM, SM] + [VM] * (2 + len(packs) + len(velocities)),
        out_specs=(VM, VM),
        scratch_shapes=[
            pltpu.VMEM((blocks, BLK, 96), BF16),
            pltpu.VMEM((window, 96, 2 * BLK), BF16),
            pltpu.VMEM((blocks, BLK, BLK), F32),
        ],
        compiler_params=params(16),
        name="nearness",
    )(targets, sources, near_sources, centre_sources, *packs, *velocities)
    return vel, near.reshape(seg)


def solution(mesh):
    in_specs = (
        P(None, "cells"),
        P(None, "cells"),
        P(None, "cells"),
        P("cells", "lanes"),
        P(None, "cells"),
        P(None, "cells"),
        P("cells"),
        P("cells"),
        P("cells"),
    )
    out_specs = (P(None, "cells"), P("cells"))
    return jax.shard_map(local, mesh=mesh, in_specs=in_specs, out_specs=out_specs, check_vma=False)
```

```python
import functools
import math

import jax
import jax.numpy as jnp
from jax import lax
from jax.experimental import pallas as pl
from jax.experimental.pallas import tpu as pltpu
from jax.sharding import PartitionSpec as P

BLK = 128
FIELDS = 9
GROUP = 8
REACH = 2
FORCE_SCALE = 0.02
CORE_SQUARE = 0.25
TIME_STEP = 4.0
MIDDLE = 2.0
LOG2E = math.log2(math.e)

F32 = jnp.float32
BF16 = jnp.bfloat16
VM = pl.BlockSpec(memory_space=pltpu.VMEM)
SM = pl.BlockSpec(memory_space=pltpu.SMEM)


def long_call():
    return pl.CostEstimate(flops=1 << 28, bytes_accessed=1 << 23, transcendentals=0)


def params(mib):
    return pltpu.CompilerParams(vmem_limit_bytes=mib << 20)


def shifted(block, cell_step, lane_step):
    cells, lanes = lax.axis_size("cells"), lax.axis_size("lanes")
    route = []
    for c in range(cells):
        for l in range(lanes):
            source = ((c + cell_step) % cells) * lanes + (l + lane_step) % lanes
            route.append((source, c * lanes + l))
    return lax.ppermute(block, ("cells", "lanes"), route)


def split3(x):
    high = x.astype(BF16).astype(F32)
    rest = x - high
    mid = rest.astype(BF16).astype(F32)
    return high, mid, rest - mid


def row(ref, field, k):
    blocks = ref.shape[0] // FIELDS
    return ref[pl.ds(field * blocks + k, 8, stride=0), :]


def rows_at(ref, field, k):
    blocks = ref.shape[0] // FIELDS
    return ref[pl.ds(field * blocks + k, 8, stride=blocks), :]


def cross(a, b):
    return [
        a[1] * b[2] - a[2] * b[1],
        a[2] * b[0] - a[0] * b[2],
        a[0] * b[1] - a[1] * b[0],
    ]


def dot3(a, b):
    return a[0] * b[0] + a[1] * b[1] + a[2] * b[2]


def choose(rows, values, other):
    for number, value in values.items():
        other = jnp.where(rows == number, value, other)
    return other


def contract_lanes(a, b):
    return lax.dot_general(a, b, (((1,), (1,)), ((), ())), preferred_element_type=F32)


def end_address(ref, first, end, k, high_count):
    node = ref[first + end, pl.ds(k, 8, stride=0), :].astype(jnp.int32)
    owner = ref[first + 2 + end, pl.ds(k, 8, stride=0), :].astype(jnp.int32)
    return owner * high_count + lax.shift_right_logical(node, BLK.bit_length() - 1), node & (BLK - 1)


def compact(entries, keep, base, discard, t_list, w_list):
    place = jnp.int32(0)
    for t, w in entries:
        t_list[place] = t
        w_list[place] = w - base
        place = place + keep(w).astype(jnp.int32)
    for u in range(GROUP):
        t_list[place + u] = jnp.int32(discard)
        w_list[place + u] = jnp.int32(0)
    return lax.div(place + (GROUP - 1), jnp.int32(GROUP))


def six_left(x):
    h, m, l = split3(x)
    return jnp.concatenate([h, h, m, h, l, m], 0)


def right_order(parts):
    h, m, l = parts
    return jnp.concatenate([h, m, h, l, h, m], 0).astype(BF16)


def pack_kernel(fields, out, numbers):
    blocks = fields.shape[1] // BLK
    for k in range(blocks):
        piece = fields[:, k * BLK : (k + 1) * BLK]
        rows = lax.broadcasted_iota(jnp.int32, piece.shape, 0)
        moved = jnp.where(rows < 3, piece - MIDDLE, piece)
        out[pl.ds(k, FIELDS, stride=blocks), :] = moved[0:FIELDS]
        for n in range(4):
            numbers[n, k : k + 1, :] = piece[FIELDS + n : FIELDS + n + 1]


def early_kernel(high_count, own, numbers, *refs):
    count = (len(refs) - 2) // 2
    for source, out in zip(refs[:count], refs[count : 2 * count]):
        out[...] = source[...]
    lhs_out, onehots = refs[2 * count :]
    rows = lax.broadcasted_iota(jnp.int32, (8, BLK), 0)
    nodes = lax.broadcasted_iota(jnp.int32, (BLK, BLK), 0)
    for k in range(own.shape[0] // FIELDS):
        c = [row(own, x, k) for x in range(3)]
        l = {3 + x: row(own, 6 + x, k) for x in range(3)}
        target = choose(rows, {**l, 6: 1.0, 7: dot3(c, c) + CORE_SQUARE}, rows_at(own, 0, k))
        lhs_out[k] = six_left(target).T
        for end in range(2):
            low = end_address(numbers, 0, end, k, high_count)[1]
            onehots[end, :, k * BLK : (k + 1) * BLK] = (nodes == low[0:1]).astype(F32).astype(BF16)


def force_tiles(lists, lhs, packs, keep, base, lhs_s, rhs_s, src_s, acc_s, t_list, w_list):
    blocks = lhs.shape[0]
    rows = lax.broadcasted_iota(jnp.int32, (8, BLK), 0)
    acc_s[...] = jnp.zeros_like(acc_s)
    entries = ((jnp.int32(t), lists[t, e]) for t in range(blocks) for e in range(lists.shape[1]))
    groups = compact(entries, keep, base, blocks, t_list, w_list)
    for t in range(blocks):
        lhs_s[t] = lhs[t].astype(BF16)
    for d, ref in enumerate(packs):
        for k in range(blocks):
            c = [row(ref, x, k) for x in range(3)]
            l = [row(ref, 6 + x, k) for x in range(3)]
            upper, lower = rows_at(ref, 0, k), rows_at(ref, 1, k)
            near = jnp.where(rows < 3, -2.0 * upper, choose(rows, {6: dot3(c, c), 7: 1.0}, 0.0))
            along = jnp.where((rows >= 3) & (rows < 6), upper, 0.0)
            moment = cross(l, c)
            sums = choose(rows, {1 + x: moment[x] for x in range(3)}, lower)
            w = d * blocks + k
            rhs_s[w, :, 0:BLK] = right_order(split3(near))
            rhs_s[w, :, BLK : 2 * BLK] = right_order(split3(along))
            src_s[w] = jnp.concatenate([*split3(sums), jnp.zeros((8, BLK), F32)], 0).astype(BF16)

    def some_tiles(step, carry):
        for u in range(GROUP):
            t = t_list[step * GROUP + u]
            w = w_list[step * GROUP + u]
            both = jnp.dot(
                lhs_s[jnp.minimum(t, blocks - 1)], rhs_s[w], preferred_element_type=F32
            )
            inverse = lax.rsqrt(both[:, :BLK])
            weight = both[:, BLK:] * inverse * (inverse * inverse)
            high = weight.astype(BF16)
            low = (weight - high.astype(F32)).astype(BF16)
            src = src_s[w]
            acc_s[t] += contract_lanes(
                jnp.concatenate([high, low], 1), jnp.concatenate([src, src], 1)
            )
        return carry

    lax.fori_loop(0, groups, some_tiles, 0)


def first_forces(lists, lhs, *refs):
    packs, acc_out, scratch = refs[: REACH + 1], refs[REACH + 1], refs[REACH + 2 :]
    lhs_s, rhs_s, src_s, t_list, w_list = scratch
    base = REACH * lhs.shape[0]
    force_tiles(
        lists, lhs, packs, lambda w: w >= base, base, lhs_s, rhs_s, src_s, acc_out, t_list, w_list
    )


def last_forces(lanes, high_count, lists, lhs, onehots, numbers, own, first_acc, *refs):
    packs, (own_out, next_out), scratch = refs[:REACH], refs[REACH : REACH + 2], refs[REACH + 2 :]
    lhs_s, rhs_s, src_s, acc_s, force_s, t_list, w_list = scratch
    blocks = lhs.shape[0]
    base = REACH * blocks
    rows = lax.broadcasted_iota(jnp.int32, (8, BLK), 0)
    force_tiles(
        lists, lhs, packs, lambda w: w < base, 0, lhs_s, rhs_s, src_s, acc_s, t_list, w_list
    )
    for t in range(blocks):
        total = (first_acc[t] + acc_s[t]).T
        force_s[t] = total[0:8] + (total[8:16] + total[16:24])

    out = None
    for k in range(blocks):
        whole = force_s.at[k]
        line = [whole[pl.ds(5 + x, 8, stride=0), :] for x in range(3)]
        moment = [whole[pl.ds(1 + x, 8, stride=0), :] for x in range(3)]
        c = [row(own, x, k) for x in range(3)]
        l = [row(own, 6 + x, k) for x in range(3)]
        turned = cross(line, c)
        values = [(0.5 * FORCE_SCALE) * (turned[x] - moment[x]) for x in range(3)]
        values.append(jnp.sqrt(dot3(l, l)) * (0.5 / lanes))
        tops = [value.astype(BF16).astype(F32) for value in values]
        parts = tops + [value - top for value, top in zip(values, tops)]
        pieces = []
        for end in range(2):
            high = end_address(numbers, 0, end, k, high_count)[0]
            masks = [rows + first == high for first in range(0, 2 * high_count, 8)]
            pieces.append([jnp.where(mask, part, 0.0) for part in parts for mask in masks])
        left = jnp.concatenate([jnp.concatenate(p, 0) for p in pieces], 1).astype(BF16)
        cut = slice(k * BLK, (k + 1) * BLK)
        term = contract_lanes(left, jnp.concatenate([onehots[end, :, cut] for end in range(2)], 1))
        out = term if out is None else out + term
    n = 8 * high_count
    out = out[0:n] + out[n : 2 * n]
    for k in range(4):
        first = 2 * high_count * k
        own_out[k] = out[first : first + high_count]
        next_out[k] = out[first + high_count : first + 2 * high_count]


def select_kernel(*refs):
    packs, (near_out, centre_out) = refs[:-2], refs[-2:]
    blocks = packs[0].shape[0] // FIELDS
    rows = lax.broadcasted_iota(jnp.int32, (8, BLK), 0)
    for d, ref in enumerate(packs):
        for k in range(blocks):
            w = d * blocks + k
            c = [row(ref, x, k) for x in range(3)]
            centre = LOG2E * rows_at(ref, 0, k)
            extra = choose(rows, {6: LOG2E * dot3(c, c), 7: LOG2E}, 0.0)
            near_out[w] = right_order(split3(jnp.where(rows < 3, -2.0 * centre, extra)))
            parts = split3(jnp.where(rows < 3, centre, choose(rows, {6: -LOG2E}, 0.0)))
            centre_out[w] = jnp.concatenate(parts, 0)


def near_tiles(
    high_count, targets, sources, keep, first_domain, near_s, centre_s, packs, nodes, make_target,
    tgt_s, src_s, acc_s, t_list, w_list,
):
    blocks = packs[0].shape[0] // FIELDS
    base = first_domain * blocks
    rows = lax.broadcasted_iota(jnp.int32, (8, BLK), 0)
    acc_s[...] = jnp.zeros_like(acc_s)
    entries = ((targets[0, k], sources[0, k]) for k in range(targets.shape[1]))
    groups = compact(entries, keep, base, blocks, t_list, w_list)
    zero = jnp.zeros((8, BLK), F32)
    nothing = jnp.zeros((48, BLK), BF16)
    signs = choose(rows, {4: -LOG2E}, zero + LOG2E)
    turn = jnp.where(rows < 3, -2.0, choose(rows, {3: 1.0}, zero))
    constant = split3(choose(rows, {5: LOG2E}, zero))
    for d, ref in enumerate(packs):
        for k in range(blocks):
            w = d * blocks + k
            v = [zero] * 3
            for end in range(2):
                high, low = end_address(nodes[d], 3, end, k, high_count)
                for owner in range(2):
                    for first in range(0, high_count, 8):
                        mask = rows + (owner * high_count + first) == high
                        for x in range(3):
                            table = nodes[d + owner][x, first : first + 8, :]
                            got = jnp.take_along_axis(table, low, axis=1, mode="promise_in_bounds")
                            v[x] = v[x] + jnp.where(mask, got, 0.0)
            for x in range(3):
                for shift in (4, 2, 1):
                    v[x] = v[x] + pltpu.roll(v[x], shift, 0)
                v[x] = v[x] * (0.5 * TIME_STEP)
            c = [row(ref, x, k) for x in range(3)]
            vv, cv = dot3(v, v), dot3(c, v)
            moved = choose(rows, {0: v[0], 1: v[1], 2: v[2], 3: vv}, cv)
            parts = split3(moved * signs)
            centre = centre_s[base + w]
            still = [centre[8 * n : 8 * n + 8] for n in range(3)]
            src_s[w, 0:48, 0:BLK] = right_order([jnp.where(rows < 3, p, 0.0) for p in parts])
            src_s[w, 48:96, 0:BLK] = right_order(
                [jnp.where(rows == 4, p, q) for p, q in zip(parts, still)]
            )
            src_s[w, 0:48, BLK : 2 * BLK] = nothing
            src_s[w, 48:96, BLK : 2 * BLK] = right_order(
                [p * turn + q for p, q in zip(parts, constant)]
            )
            if make_target is not None and d == 0:
                first = choose(rows, {6: 1.0, 7: dot3(c, c)}, rows_at(ref, 0, k))
                second = choose(rows, {3: 1.0, 4: 1.0, 5: vv, 6: cv, 7: 0.0}, moved)
                make_target(k, jnp.concatenate([six_left(first), six_left(second)], 0).T)

    def some_pairs(step, carry):
        for u in range(GROUP):
            t = t_list[step * GROUP + u]
            w = w_list[step * GROUP + u]
            target = tgt_s[jnp.minimum(t, blocks - 1)]
            rr = jnp.dot(target[:, 0:48], near_s[base + w], preferred_element_type=F32)
            both = jnp.dot(target, src_s[w], preferred_element_type=F32)
            toward = both[:, 0:BLK]
            square = jnp.maximum(both[:, BLK : 2 * BLK], 0.0)
            s = jnp.clip(toward / (square + LOG2E * CORE_SQUARE), 0.0, 1.0)
            acc_s[t] += jnp.exp2(s * (toward + (toward - s * square)) - rr)
        return carry

    lax.fori_loop(0, groups, some_pairs, 0)


def first_near(high_count, targets, sources, near_s, centre_s, *refs):
    packs, nodes = refs[: REACH + 1], refs[REACH + 1 : 2 * REACH + 3]
    acc_out, tgt_out, vel_out, tgt_s, src_s, t_list, w_list = refs[2 * REACH + 3 :]
    base = REACH * (packs[0].shape[0] // FIELDS)
    for k in range(high_count):
        for x in range(3):
            vel_out[x : x + 1, k * BLK : (k + 1) * BLK] = nodes[0][x, k : k + 1, :]

    def make_target(k, value):
        tgt_out[k] = value
        tgt_s[k] = value.astype(BF16)

    near_tiles(
        high_count, targets, sources, lambda w: w >= base, REACH, near_s, centre_s, packs, nodes,
        make_target, tgt_s, src_s, acc_out, t_list, w_list,
    )


def last_near(high_count, targets, sources, near_s, centre_s, first_acc, tgt, *refs):
    packs, nodes = refs[:REACH], refs[REACH : 2 * REACH + 1]
    near_out, tgt_s, src_s, acc_s, t_list, w_list = refs[2 * REACH + 1 :]
    blocks = tgt.shape[0]
    for t in range(blocks):
        tgt_s[t] = tgt[t].astype(BF16)
    near_tiles(
        high_count, targets, sources, lambda w: w < REACH * blocks, 0, near_s, centre_s, packs, nodes,
        None, tgt_s, src_s, acc_s, t_list, w_list,
    )
    for t in range(blocks):
        near_out[t : t + 1] = jnp.sum((first_acc[t] + acc_s[t]).T, axis=0, keepdims=True)


def velocity_kernel(mobility, numbers, *refs):
    out = refs[-1]
    total = refs[0][...]
    for ref in refs[1:-1]:
        total = total + ref[...]
    scale = mobility[...] / (1.0 + total[3])
    for x in range(3):
        out[x] = total[x] * scale
    out[3:7] = numbers[...]


def rows_of(pieces, first, rows):
    total = None
    for piece in pieces:
        last = first + piece.shape[0]
        padded = jnp.pad(piece, ((first, rows - last), (0, 0)))
        total = padded if total is None else total + padded
        first = last
    return total


def local(
    centres, seg_lines, burgers, neighbour_blocks, seg_nodes, node_owner, mobility, cand_target, cand_source
):
    seg = centres.shape[1]
    blocks = seg // BLK
    high_count = mobility.shape[0] // BLK
    lanes = lax.axis_size("lanes")
    window = (2 * REACH + 1) * blocks
    fields = rows_of([centres, burgers, seg_lines], 0, FIELDS + 4)
    fields = fields + rows_of([seg_nodes, node_owner], FIELDS, FIELDS + 4).astype(F32)
    own, numbers = pl.pallas_call(
        pack_kernel,
        out_shape=(
            jax.ShapeDtypeStruct((FIELDS * blocks, BLK), F32),
            jax.ShapeDtypeStruct((4, blocks, BLK), F32),
        ),
        in_specs=[VM],
        out_specs=(VM, VM),
        compiler_params=params(4),
        name="pack",
    )(fields)
    packs = [own if o == 0 else shifted(own, o, 0) for o in range(-REACH, REACH + 1)]
    small = [
        neighbour_blocks,
        mobility.reshape(high_count, BLK),
        cand_target.reshape(1, -1),
        cand_source.reshape(1, -1),
    ]
    lists, rate, targets, sources, lhs, own_onehots = pl.pallas_call(
        functools.partial(early_kernel, high_count),
        out_shape=[jax.ShapeDtypeStruct(x.shape, x.dtype) for x in small]
        + [
            jax.ShapeDtypeStruct((blocks, BLK, 48), F32),
            jax.ShapeDtypeStruct((2, BLK, seg), BF16),
        ],
        in_specs=[VM] * (2 + len(small)),
        out_specs=[VM] * (2 + len(small)),
        compiler_params=params(8),
        cost_estimate=long_call(),
        name="early",
    )(own, numbers, *small)

    entry_room = pltpu.SMEM((lists.shape[0] * lists.shape[1] + GROUP,), jnp.int32)
    accumulator = (blocks + 1, BLK, 32)

    def force_scratch(domains):
        return [
            pltpu.VMEM((blocks, BLK, 48), BF16),
            pltpu.VMEM((domains * blocks, 48, 2 * BLK), BF16),
            pltpu.VMEM((domains * blocks, 32, BLK), BF16),
        ]

    first_acc = pl.pallas_call(
        first_forces,
        out_shape=jax.ShapeDtypeStruct(accumulator, F32),
        in_specs=[SM] + [VM] * (2 + REACH),
        out_specs=VM,
        scratch_shapes=force_scratch(REACH + 1) + [entry_room] * 2,
        compiler_params=params(16),
        cost_estimate=long_call(),
        name="first_forces",
    )(lists, lhs, *packs[REACH:])
    part = jax.ShapeDtypeStruct((4, high_count, BLK), F32)
    own_part, next_part = pl.pallas_call(
        functools.partial(last_forces, lanes, high_count),
        out_shape=(part, part),
        in_specs=[SM] + [VM] * (5 + REACH),
        out_specs=(VM, VM),
        scratch_shapes=force_scratch(REACH)
        + [pltpu.VMEM(accumulator, F32), pltpu.VMEM((blocks, 8, BLK), F32)]
        + [entry_room] * 2,
        compiler_params=params(16),
        name="last_forces",
    )(lists, lhs, own_onehots, numbers, own, first_acc, *packs[:REACH])
    terms = [own_part]
    terms += [shifted(own_part, 0, lane) for lane in range(1, lanes)]
    terms += [shifted(next_part, -1, lane) for lane in range(lanes)]
    velocity = pl.pallas_call(
        velocity_kernel,
        out_shape=jax.ShapeDtypeStruct((7, high_count, BLK), F32),
        in_specs=[VM] * (2 + len(terms)),
        out_specs=VM,
        compiler_params=params(4),
        name="velocity",
    )(rate, numbers, *terms)
    nodes = [
        velocity if o == 0 else shifted(velocity, o, 0) for o in range(-REACH, REACH + 2)
    ]
    near_sources, centre_sources = pl.pallas_call(
        select_kernel,
        out_shape=(
            jax.ShapeDtypeStruct((window, 48, BLK), BF16),
            jax.ShapeDtypeStruct((window, 24, BLK), F32),
        ),
        in_specs=[VM] * len(packs),
        out_specs=(VM, VM),
        compiler_params=params(16),
        cost_estimate=long_call(),
        name="select",
    )(*packs)

    pair_room = pltpu.SMEM((targets.shape[1] + GROUP,), jnp.int32)
    accumulator = (blocks + 1, BLK, BLK)

    def near_scratch(domains):
        return [
            pltpu.VMEM((blocks, BLK, 96), BF16),
            pltpu.VMEM((domains * blocks, 96, 2 * BLK), BF16),
        ]

    first_sum, target_rows, vel = pl.pallas_call(
        functools.partial(first_near, high_count),
        out_shape=(
            jax.ShapeDtypeStruct(accumulator, F32),
            jax.ShapeDtypeStruct((blocks, BLK, 96), F32),
            jax.ShapeDtypeStruct((3, high_count * BLK), F32),
        ),
        in_specs=[SM, SM] + [VM] * (5 + 2 * REACH),
        out_specs=(VM, VM, VM),
        scratch_shapes=near_scratch(REACH + 1) + [pair_room] * 2,
        compiler_params=params(16),
        cost_estimate=long_call(),
        name="first_near",
    )(targets, sources, near_sources, centre_sources, *packs[REACH:], *nodes[REACH:])
    near = pl.pallas_call(
        functools.partial(last_near, high_count),
        out_shape=jax.ShapeDtypeStruct((blocks, BLK), F32),
        in_specs=[SM, SM] + [VM] * (5 + 2 * REACH),
        out_specs=VM,
        scratch_shapes=near_scratch(REACH) + [pltpu.VMEM(accumulator, F32)] + [pair_room] * 2,
        compiler_params=params(16),
        name="last_near",
    )(
        targets, sources, near_sources, centre_sources, first_sum, target_rows,
        *packs[:REACH], *nodes[: REACH + 1],
    )
    return vel, near.reshape(seg)


def solution(mesh):
    in_specs = (
        P(None, "cells"),
        P(None, "cells"),
        P(None, "cells"),
        P("cells", "lanes"),
        P(None, "cells"),
        P(None, "cells"),
        P("cells"),
        P("cells"),
        P("cells"),
    )
    out_specs = (P(None, "cells"), P("cells"))
    return jax.shard_map(local, mesh=mesh, in_specs=in_specs, out_specs=out_specs, check_vma=False)
```

```python
import functools
import math

import jax
import jax.numpy as jnp
from jax import lax
from jax.experimental import pallas as pl
from jax.experimental.pallas import tpu as pltpu
from jax.sharding import PartitionSpec as P


BLK = 128
FIELDS = 9
GROUP = 16
REACH = 2
FORCE_SCALE = 0.02
CORE_SQUARE = 0.25
TIME_STEP = 4.0
MIDDLE = 2.0
LOG2E = math.log2(math.e)

F32 = jnp.float32
BF16 = jnp.bfloat16
VM = pl.BlockSpec(memory_space=pltpu.VMEM)
SM = pl.BlockSpec(memory_space=pltpu.SMEM)


def long_call():
    return pl.CostEstimate(flops=1 << 28, bytes_accessed=1 << 23, transcendentals=0)


def params(mib):
    return pltpu.CompilerParams(vmem_limit_bytes=mib << 20)


def shifted(block, *steps):
    cell_step, lane_step = (*steps, 0)[:2]
    cells, lanes = lax.axis_size("cells"), lax.axis_size("lanes")
    route = []
    for c in range(cells):
        for l in range(lanes):
            source = ((c + cell_step) % cells) * lanes + (l + lane_step) % lanes
            route.append((source, c * lanes + l))
    return lax.ppermute(block, ("cells", "lanes"), route)


def split3(x):
    high = x.astype(BF16).astype(F32)
    rest = x - high
    mid = rest.astype(BF16).astype(F32)
    return high, mid, rest - mid


def row(ref, field, k):
    blocks = ref.shape[0] // FIELDS
    return ref[pl.ds(field * blocks + k, 8, stride=0), :]


def rows_at(ref, field, k):
    blocks = ref.shape[0] // FIELDS
    return ref[pl.ds(field * blocks + k, 8, stride=blocks), :]


def cross(a, b):
    return [
        a[1] * b[2] - a[2] * b[1],
        a[2] * b[0] - a[0] * b[2],
        a[0] * b[1] - a[1] * b[0],
    ]


def dot3(a, b):
    return a[0] * b[0] + a[1] * b[1] + a[2] * b[2]


def choose(rows, values, other):
    for number, value in values.items():
        other = jnp.where(rows == number, value, other)
    return other


def contract_lanes(a, b):
    return lax.dot_general(a, b, (((1,), (1,)), ((), ())), preferred_element_type=F32)


def end_address(ref, first, end, k, high_count):
    node = ref[first + end, pl.ds(k, 8, stride=0), :].astype(jnp.int32)
    owner = ref[first + 2 + end, pl.ds(k, 8, stride=0), :].astype(jnp.int32)
    return owner * high_count + lax.shift_right_logical(node, BLK.bit_length() - 1), node & (BLK - 1)


def compact(entries, keep, base, discard, t_list, w_list):
    place = jnp.int32(0)
    for t, w in entries:
        t_list[place] = t
        w_list[place] = w - base
        place = place + keep(w).astype(jnp.int32)
    for u in range(GROUP):
        t_list[place + u] = jnp.int32(discard)
        w_list[place + u] = jnp.int32(0)
    return lax.div(place + (GROUP - 1), jnp.int32(GROUP))


def six_left(x):
    h, m, l = split3(x)
    return jnp.concatenate([h, h, m, h, l, m], 0)


def right_order(parts):
    h, m, l = parts
    return jnp.concatenate([h, m, h, l, h, m], 0).astype(BF16)


def pack_kernel(fields, out, numbers):
    blocks = fields.shape[1] // BLK
    for k in range(blocks):
        piece = fields[:, k * BLK : (k + 1) * BLK]
        rows = lax.broadcasted_iota(jnp.int32, piece.shape, 0)
        moved = jnp.where(rows < 3, piece - MIDDLE, piece)
        out[pl.ds(k, FIELDS, stride=blocks), :] = moved[0:FIELDS]
        for n in range(4):
            numbers[n, k : k + 1, :] = piece[FIELDS + n : FIELDS + n + 1]


def early_kernel(high_count, own, numbers, *refs):
    count = (len(refs) - 2) // 2
    for source, out in zip(refs[:count], refs[count : 2 * count]):
        out[...] = source[...]
    lhs_out, onehots = refs[2 * count :]
    rows = lax.broadcasted_iota(jnp.int32, (8, BLK), 0)
    nodes = lax.broadcasted_iota(jnp.int32, (BLK, BLK), 0)
    for k in range(own.shape[0] // FIELDS):
        c = [row(own, x, k) for x in range(3)]
        l = {3 + x: row(own, 6 + x, k) for x in range(3)}
        target = choose(rows, {**l, 6: 1.0, 7: dot3(c, c) + CORE_SQUARE}, rows_at(own, 0, k))
        lhs_out[k] = six_left(target).T
        for end in range(2):
            low = end_address(numbers, 0, end, k, high_count)[1]
            onehots[end, :, k * BLK : (k + 1) * BLK] = (nodes == low[0:1]).astype(F32).astype(BF16)


def force_tiles(lists, lhs, packs, keep, base, lhs_s, rhs_s, src_s, acc_s, t_list, w_list):
    blocks = lhs.shape[0]
    rows = lax.broadcasted_iota(jnp.int32, (8, BLK), 0)
    acc_s[...] = jnp.zeros_like(acc_s)
    entries = ((jnp.int32(t), lists[t, e]) for t in range(blocks) for e in range(lists.shape[1]))
    groups = compact(entries, keep, base, blocks, t_list, w_list)
    for t in range(blocks):
        lhs_s[t] = lhs[t].astype(BF16)
    for d, ref in enumerate(packs):
        for k in range(blocks):
            c = [row(ref, x, k) for x in range(3)]
            l = [row(ref, 6 + x, k) for x in range(3)]
            upper, lower = rows_at(ref, 0, k), rows_at(ref, 1, k)
            near = jnp.where(rows < 3, -2.0 * upper, choose(rows, {6: dot3(c, c), 7: 1.0}, 0.0))
            along = jnp.where((rows >= 3) & (rows < 6), upper, 0.0)
            moment = cross(l, c)
            sums = choose(rows, {1 + x: moment[x] for x in range(3)}, lower)
            w = d * blocks + k
            rhs_s[w, :, 0:BLK] = right_order(split3(near))
            rhs_s[w, :, BLK : 2 * BLK] = right_order(split3(along))
            src_s[w] = jnp.concatenate([*split3(sums), jnp.zeros((8, BLK), F32)], 0).astype(BF16)

    def some_tiles(step, carry):
        for u in range(GROUP):
            t = t_list[step * GROUP + u]
            w = w_list[step * GROUP + u]
            both = jnp.dot(
                lhs_s[jnp.minimum(t, blocks - 1)], rhs_s[w], preferred_element_type=F32
            )
            inverse = lax.rsqrt(both[:, :BLK])
            weight = both[:, BLK:] * inverse * (inverse * inverse)
            high = weight.astype(BF16)
            low = (weight - high.astype(F32)).astype(BF16)
            src = src_s[w]
            acc_s[t] += contract_lanes(
                jnp.concatenate([high, low], 1), jnp.concatenate([src, src], 1)
            )
        return carry

    lax.fori_loop(0, groups, some_tiles, 0)


def first_forces(lists, lhs, *refs):
    packs, acc_out, scratch = refs[: REACH + 1], refs[REACH + 1], refs[REACH + 2 :]
    lhs_s, rhs_s, src_s, t_list, w_list = scratch
    base = REACH * lhs.shape[0]
    force_tiles(
        lists, lhs, packs, lambda w: w >= base, base, lhs_s, rhs_s, src_s, acc_out, t_list, w_list
    )


def last_forces(lanes, high_count, lists, lhs, onehots, numbers, own, first_acc, *refs):
    packs, (own_out, next_out), scratch = refs[:REACH], refs[REACH : REACH + 2], refs[REACH + 2 :]
    lhs_s, rhs_s, src_s, acc_s, force_s, t_list, w_list = scratch
    blocks = lhs.shape[0]
    base = REACH * blocks
    rows = lax.broadcasted_iota(jnp.int32, (8, BLK), 0)
    force_tiles(
        lists, lhs, packs, lambda w: w < base, 0, lhs_s, rhs_s, src_s, acc_s, t_list, w_list
    )
    for t in range(blocks):
        total = (first_acc[t] + acc_s[t]).T
        force_s[t] = total[0:8] + (total[8:16] + total[16:24])

    out = None
    for k in range(blocks):
        whole = force_s.at[k]
        line = [whole[pl.ds(5 + x, 8, stride=0), :] for x in range(3)]
        moment = [whole[pl.ds(1 + x, 8, stride=0), :] for x in range(3)]
        c = [row(own, x, k) for x in range(3)]
        l = [row(own, 6 + x, k) for x in range(3)]
        turned = cross(line, c)
        values = [(0.5 * FORCE_SCALE) * (turned[x] - moment[x]) for x in range(3)]
        values.append(jnp.sqrt(dot3(l, l)) * (0.5 / lanes))
        tops = [value.astype(BF16).astype(F32) for value in values]
        parts = tops + [value - top for value, top in zip(values, tops)]
        pieces = []
        for end in range(2):
            high = end_address(numbers, 0, end, k, high_count)[0]
            masks = [rows + first == high for first in range(0, 2 * high_count, 8)]
            pieces.append([jnp.where(mask, part, 0.0) for part in parts for mask in masks])
        left = jnp.concatenate([jnp.concatenate(p, 0) for p in pieces], 1).astype(BF16)
        cut = slice(k * BLK, (k + 1) * BLK)
        term = contract_lanes(left, jnp.concatenate([onehots[end, :, cut] for end in range(2)], 1))
        out = term if out is None else out + term
    n = 8 * high_count
    out = out[0:n] + out[n : 2 * n]
    for k in range(4):
        first = 2 * high_count * k
        own_out[k] = out[first : first + high_count]
        next_out[k] = out[first + high_count : first + 2 * high_count]


def select_kernel(*refs):
    packs, (near_out, centre_out) = refs[:-2], refs[-2:]
    blocks = packs[0].shape[0] // FIELDS
    rows = lax.broadcasted_iota(jnp.int32, (8, BLK), 0)
    for d, ref in enumerate(packs):
        for k in range(blocks):
            w = d * blocks + k
            c = [row(ref, x, k) for x in range(3)]
            centre = LOG2E * rows_at(ref, 0, k)
            extra = choose(rows, {6: LOG2E * dot3(c, c), 7: LOG2E}, 0.0)
            near_out[w] = right_order(split3(jnp.where(rows < 3, -2.0 * centre, extra)))
            parts = split3(jnp.where(rows < 3, centre, choose(rows, {6: -LOG2E}, 0.0)))
            centre_out[w] = jnp.concatenate(parts, 0)


def near_tiles(
    high_count, targets, sources, keep, first_domain, near_s, centre_s, packs, nodes, make_target,
    tgt_s, src_s, acc_s, t_list, w_list,
):
    blocks = packs[0].shape[0] // FIELDS
    base = first_domain * blocks
    rows = lax.broadcasted_iota(jnp.int32, (8, BLK), 0)
    acc_s[...] = jnp.zeros_like(acc_s)
    entries = ((targets[0, k], sources[0, k]) for k in range(targets.shape[1]))
    groups = compact(entries, keep, base, blocks, t_list, w_list)
    zero = jnp.zeros((8, BLK), F32)
    nothing = jnp.zeros((48, BLK), BF16)
    signs = choose(rows, {4: -LOG2E}, zero + LOG2E)
    turn = jnp.where(rows < 3, -2.0, choose(rows, {3: 1.0}, zero))
    constant = split3(choose(rows, {5: LOG2E}, zero))
    for d, ref in enumerate(packs):
        for k in range(blocks):
            w = d * blocks + k
            v = [zero] * 3
            for end in range(2):
                high, low = end_address(nodes[d], 3, end, k, high_count)
                for owner in range(2):
                    for first in range(0, high_count, 8):
                        mask = rows + (owner * high_count + first) == high
                        for x in range(3):
                            table = nodes[d + owner][x, first : first + 8, :]
                            got = jnp.take_along_axis(table, low, axis=1, mode="promise_in_bounds")
                            v[x] = v[x] + jnp.where(mask, got, 0.0)
            for x in range(3):
                for shift in (4, 2, 1):
                    v[x] = v[x] + pltpu.roll(v[x], shift, 0)
                v[x] = v[x] * (0.5 * TIME_STEP)
            c = [row(ref, x, k) for x in range(3)]
            vv, cv = dot3(v, v), dot3(c, v)
            moved = choose(rows, {0: v[0], 1: v[1], 2: v[2], 3: vv}, cv)
            parts = split3(moved * signs)
            centre = centre_s[base + w]
            still = [centre[8 * n : 8 * n + 8] for n in range(3)]
            src_s[w, 0:48, 0:BLK] = right_order([jnp.where(rows < 3, p, 0.0) for p in parts])
            src_s[w, 48:96, 0:BLK] = right_order(
                [jnp.where(rows == 4, p, q) for p, q in zip(parts, still)]
            )
            src_s[w, 0:48, BLK : 2 * BLK] = nothing
            src_s[w, 48:96, BLK : 2 * BLK] = right_order(
                [p * turn + q for p, q in zip(parts, constant)]
            )
            if make_target is not None and d == 0:
                first = choose(rows, {6: 1.0, 7: dot3(c, c)}, rows_at(ref, 0, k))
                second = choose(rows, {3: 1.0, 4: 1.0, 5: vv, 6: cv, 7: 0.0}, moved)
                make_target(k, jnp.concatenate([six_left(first), six_left(second)], 0).T)

    def some_pairs(step, carry):
        for u in range(GROUP):
            t = t_list[step * GROUP + u]
            w = w_list[step * GROUP + u]
            target = tgt_s[jnp.minimum(t, blocks - 1)]
            rr = jnp.dot(target[:, 0:48], near_s[base + w], preferred_element_type=F32)
            both = jnp.dot(target, src_s[w], preferred_element_type=F32)
            toward = both[:, 0:BLK]
            square = jnp.maximum(both[:, BLK : 2 * BLK], 0.0)
            s = jnp.clip(toward / (square + LOG2E * CORE_SQUARE), 0.0, 1.0)
            acc_s[t] += jnp.exp2(s * (toward + (toward - s * square)) - rr)
        return carry

    lax.fori_loop(0, groups, some_pairs, 0)


def first_near(high_count, targets, sources, near_s, centre_s, *refs):
    packs, nodes = refs[: REACH + 1], refs[REACH + 1 : 2 * REACH + 3]
    acc_out, tgt_out, vel_out, tgt_s, src_s, t_list, w_list = refs[2 * REACH + 3 :]
    base = REACH * (packs[0].shape[0] // FIELDS)
    for k in range(high_count):
        for x in range(3):
            vel_out[x : x + 1, k * BLK : (k + 1) * BLK] = nodes[0][x, k : k + 1, :]

    def make_target(k, value):
        tgt_out[k] = value
        tgt_s[k] = value.astype(BF16)

    near_tiles(
        high_count, targets, sources, lambda w: w >= base, REACH, near_s, centre_s, packs, nodes,
        make_target, tgt_s, src_s, acc_out, t_list, w_list,
    )


def last_near(high_count, targets, sources, near_s, centre_s, first_acc, tgt, *refs):
    packs, nodes = refs[:REACH], refs[REACH : 2 * REACH + 1]
    near_out, tgt_s, src_s, acc_s, t_list, w_list = refs[2 * REACH + 1 :]
    blocks = tgt.shape[0]
    for t in range(blocks):
        tgt_s[t] = tgt[t].astype(BF16)
    near_tiles(
        high_count, targets, sources, lambda w: w < REACH * blocks, 0, near_s, centre_s, packs, nodes,
        None, tgt_s, src_s, acc_s, t_list, w_list,
    )
    for t in range(blocks):
        near_out[t : t + 1] = jnp.sum((first_acc[t] + acc_s[t]).T, axis=0, keepdims=True)


def velocity_kernel(mobility, numbers, *refs):
    out = refs[-1]
    total = refs[0][...]
    for ref in refs[1:-1]:
        total = total + ref[...]
    scale = mobility[...] / (1.0 + total[3])
    for x in range(3):
        out[x] = total[x] * scale
    out[3:7] = numbers[...]


def rows_of(pieces, first, rows):
    total = None
    for piece in pieces:
        last = first + piece.shape[0]
        padded = jnp.pad(piece, ((first, rows - last), (0, 0)))
        total = padded if total is None else total + padded
        first = last
    return total


def local(
    centres, seg_lines, burgers, neighbour_blocks, seg_nodes, node_owner, mobility, cand_target, cand_source
):
    seg = centres.shape[1]
    blocks = seg // BLK
    high_count = mobility.shape[0] // BLK
    lanes = lax.axis_size("lanes")
    window = (2 * REACH + 1) * blocks
    fields = rows_of([centres, burgers, seg_lines], 0, FIELDS + 4)
    fields = fields + rows_of([seg_nodes, node_owner], FIELDS, FIELDS + 4).astype(F32)
    own, numbers = pl.pallas_call(
        pack_kernel,
        out_shape=(
            jax.ShapeDtypeStruct((FIELDS * blocks, BLK), F32),
            jax.ShapeDtypeStruct((4, blocks, BLK), F32),
        ),
        in_specs=[VM],
        out_specs=(VM, VM),
        compiler_params=params(4),
        name="pack",
    )(fields)
    packs = [own if o == 0 else shifted(own, o) for o in range(-REACH, REACH + 1)]
    small = [
        neighbour_blocks,
        mobility.reshape(high_count, BLK),
        cand_target.reshape(1, -1),
        cand_source.reshape(1, -1),
    ]
    lists, rate, targets, sources, lhs, own_onehots = pl.pallas_call(
        functools.partial(early_kernel, high_count),
        out_shape=[jax.ShapeDtypeStruct(x.shape, x.dtype) for x in small]
        + [
            jax.ShapeDtypeStruct((blocks, BLK, 48), F32),
            jax.ShapeDtypeStruct((2, BLK, seg), BF16),
        ],
        in_specs=[VM] * (2 + len(small)),
        out_specs=[VM] * (2 + len(small)),
        compiler_params=params(8),
        cost_estimate=long_call(),
        name="early",
    )(own, numbers, *small)

    entry_room = pltpu.SMEM((lists.shape[0] * lists.shape[1] + GROUP,), jnp.int32)
    accumulator = (blocks + 1, BLK, 32)

    def force_scratch(domains):
        return [
            pltpu.VMEM((blocks, BLK, 48), BF16),
            pltpu.VMEM((domains * blocks, 48, 2 * BLK), BF16),
            pltpu.VMEM((domains * blocks, 32, BLK), BF16),
        ]

    first_acc = pl.pallas_call(
        first_forces,
        out_shape=jax.ShapeDtypeStruct(accumulator, F32),
        in_specs=[SM] + [VM] * (2 + REACH),
        out_specs=VM,
        scratch_shapes=force_scratch(REACH + 1) + [entry_room] * 2,
        compiler_params=params(16),
        cost_estimate=long_call(),
        name="first_forces",
    )(lists, lhs, *packs[REACH:])
    part = jax.ShapeDtypeStruct((4, high_count, BLK), F32)
    own_part, next_part = pl.pallas_call(
        functools.partial(last_forces, lanes, high_count),
        out_shape=(part, part),
        in_specs=[SM] + [VM] * (5 + REACH),
        out_specs=(VM, VM),
        scratch_shapes=force_scratch(REACH)
        + [pltpu.VMEM(accumulator, F32), pltpu.VMEM((blocks, 8, BLK), F32)]
        + [entry_room] * 2,
        compiler_params=params(16),
        name="last_forces",
    )(lists, lhs, own_onehots, numbers, own, first_acc, *packs[:REACH])
    terms = [own_part]
    terms += [shifted(own_part, 0, lane) for lane in range(1, lanes)]
    terms += [shifted(next_part, -1, lane) for lane in range(lanes)]
    velocity = pl.pallas_call(
        velocity_kernel,
        out_shape=jax.ShapeDtypeStruct((7, high_count, BLK), F32),
        in_specs=[VM] * (2 + len(terms)),
        out_specs=VM,
        compiler_params=params(4),
        name="velocity",
    )(rate, numbers, *terms)
    nodes = [velocity if o == 0 else shifted(velocity, o) for o in range(-REACH, REACH + 2)]
    near_sources, centre_sources = pl.pallas_call(
        select_kernel,
        out_shape=(
            jax.ShapeDtypeStruct((window, 48, BLK), BF16),
            jax.ShapeDtypeStruct((window, 24, BLK), F32),
        ),
        in_specs=[VM] * len(packs),
        out_specs=(VM, VM),
        compiler_params=params(16),
        cost_estimate=long_call(),
        name="select",
    )(*packs)

    pair_room = pltpu.SMEM((targets.shape[1] + GROUP,), jnp.int32)
    accumulator = (blocks + 1, BLK, BLK)

    def near_scratch(domains):
        return [
            pltpu.VMEM((blocks, BLK, 96), BF16),
            pltpu.VMEM((domains * blocks, 96, 2 * BLK), BF16),
        ]

    first_sum, target_rows, vel = pl.pallas_call(
        functools.partial(first_near, high_count),
        out_shape=(
            jax.ShapeDtypeStruct(accumulator, F32),
            jax.ShapeDtypeStruct((blocks, BLK, 96), F32),
            jax.ShapeDtypeStruct((3, high_count * BLK), F32),
        ),
        in_specs=[SM, SM] + [VM] * (5 + 2 * REACH),
        out_specs=(VM, VM, VM),
        scratch_shapes=near_scratch(REACH + 1) + [pair_room] * 2,
        compiler_params=params(16),
        cost_estimate=long_call(),
        name="first_near",
    )(targets, sources, near_sources, centre_sources, *packs[REACH:], *nodes[REACH:])
    near = pl.pallas_call(
        functools.partial(last_near, high_count),
        out_shape=jax.ShapeDtypeStruct((blocks, BLK), F32),
        in_specs=[SM, SM] + [VM] * (5 + 2 * REACH),
        out_specs=VM,
        scratch_shapes=near_scratch(REACH) + [pltpu.VMEM(accumulator, F32)] + [pair_room] * 2,
        compiler_params=params(16),
        name="last_near",
    )(
        targets, sources, near_sources, centre_sources, first_sum, target_rows,
        *packs[:REACH], *nodes[: REACH + 1],
    )
    return vel, near.reshape(seg)


def solution(mesh):
    in_specs = (
        P(None, "cells"),
        P(None, "cells"),
        P(None, "cells"),
        P("cells", "lanes"),
        P(None, "cells"),
        P(None, "cells"),
        P("cells"),
        P("cells"),
        P("cells"),
    )
    out_specs = (P(None, "cells"), P("cells"))

    return jax.shard_map(local, mesh=mesh, in_specs=in_specs, out_specs=out_specs, check_vma=False)
```

```python
import functools
import math

import jax
import jax.numpy as jnp
from jax import lax
from jax.experimental import pallas as pl
from jax.experimental.pallas import tpu as pltpu
from jax.sharding import PartitionSpec as P


BLK = 128
FIELDS = 9
FORCE_GROUP = 16
NEAR_GROUP = 8
REACH = 2
FORCE_SCALE = 0.02
CORE_SQUARE = 0.25
TIME_STEP = 4.0
MIDDLE = 2.0
LOG2E = math.log2(math.e)

F32 = jnp.float32
BF16 = jnp.bfloat16
VM = pl.BlockSpec(memory_space=pltpu.VMEM)
SM = pl.BlockSpec(memory_space=pltpu.SMEM)


def long_call():
    return pl.CostEstimate(flops=1 << 28, bytes_accessed=1 << 23, transcendentals=0)


def params(mib):
    return pltpu.CompilerParams(vmem_limit_bytes=mib << 20)


def shifted(block, *steps):
    cell_step, lane_step = (*steps, 0)[:2]
    cells, lanes = lax.axis_size("cells"), lax.axis_size("lanes")
    route = []
    for c in range(cells):
        for l in range(lanes):
            source = ((c + cell_step) % cells) * lanes + (l + lane_step) % lanes
            route.append((source, c * lanes + l))
    return lax.ppermute(block, ("cells", "lanes"), route)


def split3(x):
    high = x.astype(BF16).astype(F32)
    rest = x - high
    mid = rest.astype(BF16).astype(F32)
    return high, mid, rest - mid


def row(ref, field, k):
    blocks = ref.shape[0] // FIELDS
    return ref[pl.ds(field * blocks + k, 8, stride=0), :]


def rows_at(ref, field, k):
    blocks = ref.shape[0] // FIELDS
    return ref[pl.ds(field * blocks + k, 8, stride=blocks), :]


def cross(a, b):
    return [
        a[1] * b[2] - a[2] * b[1],
        a[2] * b[0] - a[0] * b[2],
        a[0] * b[1] - a[1] * b[0],
    ]


def dot3(a, b):
    return a[0] * b[0] + a[1] * b[1] + a[2] * b[2]


def choose(rows, values, other):
    for number, value in values.items():
        other = jnp.where(rows == number, value, other)
    return other


def contract_lanes(a, b):
    return lax.dot_general(a, b, (((1,), (1,)), ((), ())), preferred_element_type=F32)


def end_address(ref, first, end, k, high_count):
    node = ref[first + end, pl.ds(k, 8, stride=0), :].astype(jnp.int32)
    owner = ref[first + 2 + end, pl.ds(k, 8, stride=0), :].astype(jnp.int32)
    return owner * high_count + lax.shift_right_logical(node, BLK.bit_length() - 1), node & (BLK - 1)


def compact(entries, keep, base, discard, group, t_list, w_list):
    place = jnp.int32(0)
    for t, w in entries:
        t_list[place] = t
        w_list[place] = w - base
        place = place + keep(w).astype(jnp.int32)
    for u in range(group):
        t_list[place + u] = jnp.int32(discard)
        w_list[place + u] = jnp.int32(0)
    return lax.div(place + (group - 1), jnp.int32(group))


def six_left(x):
    h, m, l = split3(x)
    return jnp.concatenate([h, h, m, h, l, m], 0)


def right_order(parts):
    h, m, l = parts
    return jnp.concatenate([h, m, h, l, h, m], 0).astype(BF16)


def pack_kernel(fields, out, numbers):
    blocks = fields.shape[1] // BLK
    for k in range(blocks):
        piece = fields[:, k * BLK : (k + 1) * BLK]
        rows = lax.broadcasted_iota(jnp.int32, piece.shape, 0)
        moved = jnp.where(rows < 3, piece - MIDDLE, piece)
        out[pl.ds(k, FIELDS, stride=blocks), :] = moved[0:FIELDS]
        for n in range(4):
            numbers[n, k : k + 1, :] = piece[FIELDS + n : FIELDS + n + 1]


def early_kernel(high_count, own, numbers, *refs):
    count = (len(refs) - 2) // 2
    for source, out in zip(refs[:count], refs[count : 2 * count]):
        out[...] = source[...]
    lhs_out, onehots = refs[2 * count :]
    rows = lax.broadcasted_iota(jnp.int32, (8, BLK), 0)
    nodes = lax.broadcasted_iota(jnp.int32, (BLK, BLK), 0)
    for k in range(own.shape[0] // FIELDS):
        c = [row(own, x, k) for x in range(3)]
        l = {3 + x: row(own, 6 + x, k) for x in range(3)}
        target = choose(rows, {**l, 6: 1.0, 7: dot3(c, c) + CORE_SQUARE}, rows_at(own, 0, k))
        lhs_out[k] = six_left(target).T
        for end in range(2):
            low = end_address(numbers, 0, end, k, high_count)[1]
            onehots[end, :, k * BLK : (k + 1) * BLK] = (nodes == low[0:1]).astype(F32).astype(BF16)


def force_tiles(lists, lhs, packs, keep, base, lhs_s, rhs_s, src_s, acc_s, t_list, w_list):
    blocks = lhs.shape[0]
    rows = lax.broadcasted_iota(jnp.int32, (8, BLK), 0)
    acc_s[...] = jnp.zeros_like(acc_s)
    entries = ((jnp.int32(t), lists[t, e]) for t in range(blocks) for e in range(lists.shape[1]))
    groups = compact(entries, keep, base, blocks, FORCE_GROUP, t_list, w_list)
    for t in range(blocks):
        lhs_s[t] = lhs[t].astype(BF16)
    for d, ref in enumerate(packs):
        for k in range(blocks):
            c = [row(ref, x, k) for x in range(3)]
            l = [row(ref, 6 + x, k) for x in range(3)]
            upper, lower = rows_at(ref, 0, k), rows_at(ref, 1, k)
            near = jnp.where(rows < 3, -2.0 * upper, choose(rows, {6: dot3(c, c), 7: 1.0}, 0.0))
            along = jnp.where((rows >= 3) & (rows < 6), upper, 0.0)
            moment = cross(l, c)
            sums = choose(rows, {1 + x: moment[x] for x in range(3)}, lower)
            w = d * blocks + k
            rhs_s[w, :, 0:BLK] = right_order(split3(near))
            rhs_s[w, :, BLK : 2 * BLK] = right_order(split3(along))
            src_s[w] = jnp.concatenate([*split3(sums), jnp.zeros((8, BLK), F32)], 0).astype(BF16)

    def some_tiles(step, carry):
        for u in range(FORCE_GROUP):
            t = t_list[step * FORCE_GROUP + u]
            w = w_list[step * FORCE_GROUP + u]
            both = jnp.dot(
                lhs_s[jnp.minimum(t, blocks - 1)], rhs_s[w], preferred_element_type=F32
            )
            inverse = lax.rsqrt(both[:, :BLK])
            weight = both[:, BLK:] * inverse * (inverse * inverse)
            high = weight.astype(BF16)
            low = (weight - high.astype(F32)).astype(BF16)
            src = src_s[w]
            acc_s[t] += contract_lanes(
                jnp.concatenate([high, low], 1), jnp.concatenate([src, src], 1)
            )
        return carry

    lax.fori_loop(0, groups, some_tiles, 0)


def first_forces(lists, lhs, *refs):
    packs, acc_out, scratch = refs[: REACH + 1], refs[REACH + 1], refs[REACH + 2 :]
    lhs_s, rhs_s, src_s, t_list, w_list = scratch
    base = REACH * lhs.shape[0]
    force_tiles(
        lists, lhs, packs, lambda w: w >= base, base, lhs_s, rhs_s, src_s, acc_out, t_list, w_list
    )


def last_forces(lanes, high_count, lists, lhs, onehots, numbers, own, first_acc, *refs):
    packs, (own_out, next_out), scratch = refs[:REACH], refs[REACH : REACH + 2], refs[REACH + 2 :]
    lhs_s, rhs_s, src_s, acc_s, force_s, t_list, w_list = scratch
    blocks = lhs.shape[0]
    base = REACH * blocks
    rows = lax.broadcasted_iota(jnp.int32, (8, BLK), 0)
    force_tiles(
        lists, lhs, packs, lambda w: w < base, 0, lhs_s, rhs_s, src_s, acc_s, t_list, w_list
    )
    for t in range(blocks):
        total = (first_acc[t] + acc_s[t]).T
        force_s[t] = total[0:8] + (total[8:16] + total[16:24])

    out = None
    for k in range(blocks):
        whole = force_s.at[k]
        line = [whole[pl.ds(5 + x, 8, stride=0), :] for x in range(3)]
        moment = [whole[pl.ds(1 + x, 8, stride=0), :] for x in range(3)]
        c = [row(own, x, k) for x in range(3)]
        l = [row(own, 6 + x, k) for x in range(3)]
        turned = cross(line, c)
        values = [(0.5 * FORCE_SCALE) * (turned[x] - moment[x]) for x in range(3)]
        values.append(jnp.sqrt(dot3(l, l)) * (0.5 / lanes))
        tops = [value.astype(BF16).astype(F32) for value in values]
        parts = tops + [value - top for value, top in zip(values, tops)]
        pieces = []
        for end in range(2):
            high = end_address(numbers, 0, end, k, high_count)[0]
            masks = [rows + first == high for first in range(0, 2 * high_count, 8)]
            pieces.append([jnp.where(mask, part, 0.0) for part in parts for mask in masks])
        left = jnp.concatenate([jnp.concatenate(p, 0) for p in pieces], 1).astype(BF16)
        cut = slice(k * BLK, (k + 1) * BLK)
        term = contract_lanes(left, jnp.concatenate([onehots[end, :, cut] for end in range(2)], 1))
        out = term if out is None else out + term
    n = 8 * high_count
    out = out[0:n] + out[n : 2 * n]
    for k in range(4):
        first = 2 * high_count * k
        own_out[k] = out[first : first + high_count]
        next_out[k] = out[first + high_count : first + 2 * high_count]


def select_kernel(*refs):
    packs, (near_out, centre_out) = refs[:-2], refs[-2:]
    blocks = packs[0].shape[0] // FIELDS
    rows = lax.broadcasted_iota(jnp.int32, (8, BLK), 0)
    for d, ref in enumerate(packs):
        for k in range(blocks):
            w = d * blocks + k
            c = [row(ref, x, k) for x in range(3)]
            centre = LOG2E * rows_at(ref, 0, k)
            extra = choose(rows, {6: LOG2E * dot3(c, c), 7: LOG2E}, 0.0)
            near_out[w] = right_order(split3(jnp.where(rows < 3, -2.0 * centre, extra)))
            parts = split3(jnp.where(rows < 3, centre, choose(rows, {6: -LOG2E}, 0.0)))
            centre_out[w] = jnp.concatenate(parts, 0)


def near_tiles(
    high_count, targets, sources, keep, first_domain, near_s, centre_s, packs, nodes, make_target,
    tgt_s, src_s, acc_s, t_list, w_list,
):
    blocks = packs[0].shape[0] // FIELDS
    base = first_domain * blocks
    rows = lax.broadcasted_iota(jnp.int32, (8, BLK), 0)
    acc_s[...] = jnp.zeros_like(acc_s)
    entries = ((targets[0, k], sources[0, k]) for k in range(targets.shape[1]))
    groups = compact(entries, keep, base, blocks, NEAR_GROUP, t_list, w_list)
    zero = jnp.zeros((8, BLK), F32)
    nothing = jnp.zeros((48, BLK), BF16)
    signs = choose(rows, {4: -LOG2E}, zero + LOG2E)
    turn = jnp.where(rows < 3, -2.0, choose(rows, {3: 1.0}, zero))
    constant = split3(choose(rows, {5: LOG2E}, zero))
    for d, ref in enumerate(packs):
        for k in range(blocks):
            w = d * blocks + k
            v = [zero] * 3
            for end in range(2):
                high, low = end_address(nodes[d], 3, end, k, high_count)
                for owner in range(2):
                    for first in range(0, high_count, 8):
                        mask = rows + (owner * high_count + first) == high
                        for x in range(3):
                            table = nodes[d + owner][x, first : first + 8, :]
                            got = jnp.take_along_axis(table, low, axis=1, mode="promise_in_bounds")
                            v[x] = v[x] + jnp.where(mask, got, 0.0)
            for x in range(3):
                for shift in (4, 2, 1):
                    v[x] = v[x] + pltpu.roll(v[x], shift, 0)
                v[x] = v[x] * (0.5 * TIME_STEP)
            c = [row(ref, x, k) for x in range(3)]
            vv, cv = dot3(v, v), dot3(c, v)
            moved = choose(rows, {0: v[0], 1: v[1], 2: v[2], 3: vv}, cv)
            parts = split3(moved * signs)
            centre = centre_s[base + w]
            still = [centre[8 * n : 8 * n + 8] for n in range(3)]
            src_s[w, 0:48, 0:BLK] = right_order([jnp.where(rows < 3, p, 0.0) for p in parts])
            src_s[w, 48:96, 0:BLK] = right_order(
                [jnp.where(rows == 4, p, q) for p, q in zip(parts, still)]
            )
            src_s[w, 0:48, BLK : 2 * BLK] = nothing
            src_s[w, 48:96, BLK : 2 * BLK] = right_order(
                [p * turn + q for p, q in zip(parts, constant)]
            )
            if make_target is not None and d == 0:
                first = choose(rows, {6: 1.0, 7: dot3(c, c)}, rows_at(ref, 0, k))
                second = choose(rows, {3: 1.0, 4: 1.0, 5: vv, 6: cv, 7: 0.0}, moved)
                make_target(k, jnp.concatenate([six_left(first), six_left(second)], 0).T)

    def some_pairs(step, carry):
        for u in range(NEAR_GROUP):
            t = t_list[step * NEAR_GROUP + u]
            w = w_list[step * NEAR_GROUP + u]
            target = tgt_s[jnp.minimum(t, blocks - 1)]
            rr = jnp.dot(target[:, 0:48], near_s[base + w], preferred_element_type=F32)
            both = jnp.dot(target, src_s[w], preferred_element_type=F32)
            toward = both[:, 0:BLK]
            square = jnp.maximum(both[:, BLK : 2 * BLK], 0.0)
            s = jnp.clip(toward / (square + LOG2E * CORE_SQUARE), 0.0, 1.0)
            acc_s[t] += jnp.exp2(s * (toward + (toward - s * square)) - rr)
        return carry

    lax.fori_loop(0, groups, some_pairs, 0)


def first_near(high_count, targets, sources, near_s, centre_s, *refs):
    packs, nodes = refs[: REACH + 1], refs[REACH + 1 : 2 * REACH + 3]
    acc_out, tgt_out, vel_out, tgt_s, src_s, t_list, w_list = refs[2 * REACH + 3 :]
    base = REACH * (packs[0].shape[0] // FIELDS)
    for k in range(high_count):
        for x in range(3):
            vel_out[x : x + 1, k * BLK : (k + 1) * BLK] = nodes[0][x, k : k + 1, :]

    def make_target(k, value):
        tgt_out[k] = value
        tgt_s[k] = value.astype(BF16)

    near_tiles(
        high_count, targets, sources, lambda w: w >= base, REACH, near_s, centre_s, packs, nodes,
        make_target, tgt_s, src_s, acc_out, t_list, w_list,
    )


def last_near(high_count, targets, sources, near_s, centre_s, first_acc, tgt, *refs):
    packs, nodes = refs[:REACH], refs[REACH : 2 * REACH + 1]
    near_out, tgt_s, src_s, acc_s, t_list, w_list = refs[2 * REACH + 1 :]
    blocks = tgt.shape[0]
    for t in range(blocks):
        tgt_s[t] = tgt[t].astype(BF16)
    near_tiles(
        high_count, targets, sources, lambda w: w < REACH * blocks, 0, near_s, centre_s, packs, nodes,
        None, tgt_s, src_s, acc_s, t_list, w_list,
    )
    for t in range(blocks):
        near_out[t : t + 1] = jnp.sum((first_acc[t] + acc_s[t]).T, axis=0, keepdims=True)


def velocity_kernel(mobility, numbers, *refs):
    out = refs[-1]
    total = refs[0][...]
    for ref in refs[1:-1]:
        total = total + ref[...]
    scale = mobility[...] / (1.0 + total[3])
    for x in range(3):
        out[x] = total[x] * scale
    out[3:7] = numbers[...]


def rows_of(pieces, first, rows):
    total = None
    for piece in pieces:
        last = first + piece.shape[0]
        padded = jnp.pad(piece, ((first, rows - last), (0, 0)))
        total = padded if total is None else total + padded
        first = last
    return total


def local(
    centres, seg_lines, burgers, neighbour_blocks, seg_nodes, node_owner, mobility, cand_target, cand_source
):
    seg = centres.shape[1]
    blocks = seg // BLK
    high_count = mobility.shape[0] // BLK
    lanes = lax.axis_size("lanes")
    window = (2 * REACH + 1) * blocks
    fields = rows_of([centres, burgers, seg_lines], 0, FIELDS + 4)
    fields = fields + rows_of([seg_nodes, node_owner], FIELDS, FIELDS + 4).astype(F32)
    own, numbers = pl.pallas_call(
        pack_kernel,
        out_shape=(
            jax.ShapeDtypeStruct((FIELDS * blocks, BLK), F32),
            jax.ShapeDtypeStruct((4, blocks, BLK), F32),
        ),
        in_specs=[VM],
        out_specs=(VM, VM),
        compiler_params=params(4),
        name="pack",
    )(fields)
    packs = [own if o == 0 else shifted(own, o) for o in range(-REACH, REACH + 1)]
    small = [
        neighbour_blocks,
        mobility.reshape(high_count, BLK),
        cand_target.reshape(1, -1),
        cand_source.reshape(1, -1),
    ]
    lists, rate, targets, sources, lhs, own_onehots = pl.pallas_call(
        functools.partial(early_kernel, high_count),
        out_shape=[jax.ShapeDtypeStruct(x.shape, x.dtype) for x in small]
        + [
            jax.ShapeDtypeStruct((blocks, BLK, 48), F32),
            jax.ShapeDtypeStruct((2, BLK, seg), BF16),
        ],
        in_specs=[VM] * (2 + len(small)),
        out_specs=[VM] * (2 + len(small)),
        compiler_params=params(8),
        cost_estimate=long_call(),
        name="early",
    )(own, numbers, *small)

    entry_room = pltpu.SMEM((lists.shape[0] * lists.shape[1] + FORCE_GROUP,), jnp.int32)
    accumulator = (blocks + 1, BLK, 32)

    def force_scratch(domains):
        return [
            pltpu.VMEM((blocks, BLK, 48), BF16),
            pltpu.VMEM((domains * blocks, 48, 2 * BLK), BF16),
            pltpu.VMEM((domains * blocks, 32, BLK), BF16),
        ]

    first_acc = pl.pallas_call(
        first_forces,
        out_shape=jax.ShapeDtypeStruct(accumulator, F32),
        in_specs=[SM] + [VM] * (2 + REACH),
        out_specs=VM,
        scratch_shapes=force_scratch(REACH + 1) + [entry_room] * 2,
        compiler_params=params(16),
        cost_estimate=long_call(),
        name="first_forces",
    )(lists, lhs, *packs[REACH:])
    part = jax.ShapeDtypeStruct((4, high_count, BLK), F32)
    own_part, next_part = pl.pallas_call(
        functools.partial(last_forces, lanes, high_count),
        out_shape=(part, part),
        in_specs=[SM] + [VM] * (5 + REACH),
        out_specs=(VM, VM),
        scratch_shapes=force_scratch(REACH)
        + [pltpu.VMEM(accumulator, F32), pltpu.VMEM((blocks, 8, BLK), F32)]
        + [entry_room] * 2,
        compiler_params=params(16),
        name="last_forces",
    )(lists, lhs, own_onehots, numbers, own, first_acc, *packs[:REACH])
    terms = [own_part]
    terms += [shifted(own_part, 0, lane) for lane in range(1, lanes)]
    terms += [shifted(next_part, -1, lane) for lane in range(lanes)]
    velocity = pl.pallas_call(
        velocity_kernel,
        out_shape=jax.ShapeDtypeStruct((7, high_count, BLK), F32),
        in_specs=[VM] * (2 + len(terms)),
        out_specs=VM,
        compiler_params=params(4),
        name="velocity",
    )(rate, numbers, *terms)
    nodes = [velocity if o == 0 else shifted(velocity, o) for o in range(-REACH, REACH + 2)]
    near_sources, centre_sources = pl.pallas_call(
        select_kernel,
        out_shape=(
            jax.ShapeDtypeStruct((window, 48, BLK), BF16),
            jax.ShapeDtypeStruct((window, 24, BLK), F32),
        ),
        in_specs=[VM] * len(packs),
        out_specs=(VM, VM),
        compiler_params=params(16),
        cost_estimate=long_call(),
        name="select",
    )(*packs)

    pair_room = pltpu.SMEM((targets.shape[1] + NEAR_GROUP,), jnp.int32)
    accumulator = (blocks + 1, BLK, BLK)

    def near_scratch(domains):
        return [
            pltpu.VMEM((blocks, BLK, 96), BF16),
            pltpu.VMEM((domains * blocks, 96, 2 * BLK), BF16),
        ]

    first_sum, target_rows, vel = pl.pallas_call(
        functools.partial(first_near, high_count),
        out_shape=(
            jax.ShapeDtypeStruct(accumulator, F32),
            jax.ShapeDtypeStruct((blocks, BLK, 96), F32),
            jax.ShapeDtypeStruct((3, high_count * BLK), F32),
        ),
        in_specs=[SM, SM] + [VM] * (5 + 2 * REACH),
        out_specs=(VM, VM, VM),
        scratch_shapes=near_scratch(REACH + 1) + [pair_room] * 2,
        compiler_params=params(16),
        cost_estimate=long_call(),
        name="first_near",
    )(targets, sources, near_sources, centre_sources, *packs[REACH:], *nodes[REACH:])
    near = pl.pallas_call(
        functools.partial(last_near, high_count),
        out_shape=jax.ShapeDtypeStruct((blocks, BLK), F32),
        in_specs=[SM, SM] + [VM] * (5 + 2 * REACH),
        out_specs=VM,
        scratch_shapes=near_scratch(REACH) + [pltpu.VMEM(accumulator, F32)] + [pair_room] * 2,
        compiler_params=params(16),
        name="last_near",
    )(
        targets, sources, near_sources, centre_sources, first_sum, target_rows,
        *packs[:REACH], *nodes[: REACH + 1],
    )
    return vel, near.reshape(seg)


def solution(mesh):
    in_specs = (
        P(None, "cells"),
        P(None, "cells"),
        P(None, "cells"),
        P("cells", "lanes"),
        P(None, "cells"),
        P(None, "cells"),
        P("cells"),
        P("cells"),
        P("cells"),
    )
    out_specs = (P(None, "cells"), P("cells"))

    return jax.shard_map(local, mesh=mesh, in_specs=in_specs, out_specs=out_specs, check_vma=False)
```

```python
import functools
import math

import jax
import jax.numpy as jnp
from jax import lax
from jax.experimental import pallas as pl
from jax.experimental.pallas import tpu as pltpu
from jax.sharding import PartitionSpec as P


BLK = 128
FIELDS = 9
FORCE_GROUP = 32
NEAR_GROUP = 8
REACH = 2
FORCE_SCALE = 0.02
CORE_SQUARE = 0.25
TIME_STEP = 4.0
MIDDLE = 2.0
LOG2E = math.log2(math.e)

F32 = jnp.float32
BF16 = jnp.bfloat16
VM = pl.BlockSpec(memory_space=pltpu.VMEM)
SM = pl.BlockSpec(memory_space=pltpu.SMEM)


def long_call():
    return pl.CostEstimate(flops=1 << 28, bytes_accessed=1 << 23, transcendentals=0)


def params(mib):
    return pltpu.CompilerParams(vmem_limit_bytes=mib << 20)


def shifted(block, *steps):
    cell_step, lane_step = (*steps, 0)[:2]
    cells, lanes = lax.axis_size("cells"), lax.axis_size("lanes")
    route = []
    for c in range(cells):
        for l in range(lanes):
            source = ((c + cell_step) % cells) * lanes + (l + lane_step) % lanes
            route.append((source, c * lanes + l))
    return lax.ppermute(block, ("cells", "lanes"), route)


def split3(x):
    high = x.astype(BF16).astype(F32)
    rest = x - high
    mid = rest.astype(BF16).astype(F32)
    return high, mid, rest - mid


def row(ref, field, k):
    blocks = ref.shape[0] // FIELDS
    return ref[pl.ds(field * blocks + k, 8, stride=0), :]


def rows_at(ref, field, k):
    blocks = ref.shape[0] // FIELDS
    return ref[pl.ds(field * blocks + k, 8, stride=blocks), :]


def cross(a, b):
    return [
        a[1] * b[2] - a[2] * b[1],
        a[2] * b[0] - a[0] * b[2],
        a[0] * b[1] - a[1] * b[0],
    ]


def dot3(a, b):
    return a[0] * b[0] + a[1] * b[1] + a[2] * b[2]


def choose(rows, values, other):
    for number, value in values.items():
        other = jnp.where(rows == number, value, other)
    return other


def contract_lanes(a, b):
    return lax.dot_general(a, b, (((1,), (1,)), ((), ())), preferred_element_type=F32)


def end_address(ref, first, end, k, high_count):
    node = ref[first + end, pl.ds(k, 8, stride=0), :].astype(jnp.int32)
    owner = ref[first + 2 + end, pl.ds(k, 8, stride=0), :].astype(jnp.int32)
    return owner * high_count + lax.shift_right_logical(node, BLK.bit_length() - 1), node & (BLK - 1)


def compact(entries, keep, base, discard, group, t_list, w_list):
    place = jnp.int32(0)
    for t, w in entries:
        t_list[place] = t
        w_list[place] = w - base
        place = place + keep(w).astype(jnp.int32)
    for u in range(group):
        t_list[place + u] = jnp.int32(discard)
        w_list[place + u] = jnp.int32(0)
    return place


def in_groups(count, group, work):
    half = group // 2
    wholes = lax.div(count + (half - 1), jnp.int32(group))

    def step(number, carry):
        work(number * group, group)
        return carry

    lax.fori_loop(0, wholes, step, 0)

    @pl.when(count > wholes * group)
    def _():
        work(wholes * group, half)


def six_left(x):
    h, m, l = split3(x)
    return jnp.concatenate([h, h, m, h, l, m], 0)


def right_order(parts):
    h, m, l = parts
    return jnp.concatenate([h, m, h, l, h, m], 0).astype(BF16)


def pack_kernel(fields, out, numbers):
    blocks = fields.shape[1] // BLK
    for k in range(blocks):
        piece = fields[:, k * BLK : (k + 1) * BLK]
        rows = lax.broadcasted_iota(jnp.int32, piece.shape, 0)
        moved = jnp.where(rows < 3, piece - MIDDLE, piece)
        out[pl.ds(k, FIELDS, stride=blocks), :] = moved[0:FIELDS]
        for n in range(4):
            numbers[n, k : k + 1, :] = piece[FIELDS + n : FIELDS + n + 1]


def early_kernel(high_count, own, numbers, *refs):
    count = (len(refs) - 2) // 2
    for source, out in zip(refs[:count], refs[count : 2 * count]):
        out[...] = source[...]
    lhs_out, onehots = refs[2 * count :]
    rows = lax.broadcasted_iota(jnp.int32, (8, BLK), 0)
    nodes = lax.broadcasted_iota(jnp.int32, (BLK, BLK), 0)
    for k in range(own.shape[0] // FIELDS):
        c = [row(own, x, k) for x in range(3)]
        l = {3 + x: row(own, 6 + x, k) for x in range(3)}
        target = choose(rows, {**l, 6: 1.0, 7: dot3(c, c) + CORE_SQUARE}, rows_at(own, 0, k))
        lhs_out[k] = six_left(target).T
        for end in range(2):
            low = end_address(numbers, 0, end, k, high_count)[1]
            onehots[end, :, k * BLK : (k + 1) * BLK] = (nodes == low[0:1]).astype(F32).astype(BF16)


def force_tiles(lists, lhs, packs, keep, base, lhs_s, rhs_s, src_s, acc_s, t_list, w_list):
    blocks = lhs.shape[0]
    rows = lax.broadcasted_iota(jnp.int32, (8, BLK), 0)
    acc_s[...] = jnp.zeros_like(acc_s)
    entries = ((jnp.int32(t), lists[t, e]) for t in range(blocks) for e in range(lists.shape[1]))
    count = compact(entries, keep, base, blocks, FORCE_GROUP, t_list, w_list)
    for t in range(blocks):
        lhs_s[t] = lhs[t].astype(BF16)
    for d, ref in enumerate(packs):
        for k in range(blocks):
            c = [row(ref, x, k) for x in range(3)]
            l = [row(ref, 6 + x, k) for x in range(3)]
            upper, lower = rows_at(ref, 0, k), rows_at(ref, 1, k)
            near = jnp.where(rows < 3, -2.0 * upper, choose(rows, {6: dot3(c, c), 7: 1.0}, 0.0))
            along = jnp.where((rows >= 3) & (rows < 6), upper, 0.0)
            moment = cross(l, c)
            sums = choose(rows, {1 + x: moment[x] for x in range(3)}, lower)
            w = d * blocks + k
            rhs_s[w, :, 0:BLK] = right_order(split3(near))
            rhs_s[w, :, BLK : 2 * BLK] = right_order(split3(along))
            src_s[w] = jnp.concatenate([*split3(sums), jnp.zeros((8, BLK), F32)], 0).astype(BF16)

    def some_tiles(first, number):
        for u in range(number):
            t = t_list[first + u]
            w = w_list[first + u]
            both = jnp.dot(
                lhs_s[jnp.minimum(t, blocks - 1)], rhs_s[w], preferred_element_type=F32
            )
            inverse = lax.rsqrt(both[:, :BLK])
            weight = both[:, BLK:] * inverse * (inverse * inverse)
            high = weight.astype(BF16)
            low = (weight - high.astype(F32)).astype(BF16)
            src = src_s[w]
            acc_s[t] += contract_lanes(
                jnp.concatenate([high, low], 1), jnp.concatenate([src, src], 1)
            )

    in_groups(count, FORCE_GROUP, some_tiles)


def first_forces(lists, lhs, *refs):
    packs, acc_out, scratch = refs[: REACH + 1], refs[REACH + 1], refs[REACH + 2 :]
    lhs_s, rhs_s, src_s, t_list, w_list = scratch
    base = REACH * lhs.shape[0]
    force_tiles(
        lists, lhs, packs, lambda w: w >= base, base, lhs_s, rhs_s, src_s, acc_out, t_list, w_list
    )


def last_forces(lanes, high_count, lists, lhs, onehots, numbers, own, first_acc, *refs):
    packs, (own_out, next_out), scratch = refs[:REACH], refs[REACH : REACH + 2], refs[REACH + 2 :]
    lhs_s, rhs_s, src_s, acc_s, force_s, t_list, w_list = scratch
    blocks = lhs.shape[0]
    base = REACH * blocks
    rows = lax.broadcasted_iota(jnp.int32, (8, BLK), 0)
    force_tiles(
        lists, lhs, packs, lambda w: w < base, 0, lhs_s, rhs_s, src_s, acc_s, t_list, w_list
    )
    for t in range(blocks):
        total = (first_acc[t] + acc_s[t]).T
        force_s[t] = total[0:8] + (total[8:16] + total[16:24])

    out = None
    for k in range(blocks):
        whole = force_s.at[k]
        line = [whole[pl.ds(5 + x, 8, stride=0), :] for x in range(3)]
        moment = [whole[pl.ds(1 + x, 8, stride=0), :] for x in range(3)]
        c = [row(own, x, k) for x in range(3)]
        l = [row(own, 6 + x, k) for x in range(3)]
        turned = cross(line, c)
        values = [(0.5 * FORCE_SCALE) * (turned[x] - moment[x]) for x in range(3)]
        values.append(jnp.sqrt(dot3(l, l)) * (0.5 / lanes))
        tops = [value.astype(BF16).astype(F32) for value in values]
        parts = tops + [value - top for value, top in zip(values, tops)]
        pieces = []
        for end in range(2):
            high = end_address(numbers, 0, end, k, high_count)[0]
            masks = [rows + first == high for first in range(0, 2 * high_count, 8)]
            pieces.append([jnp.where(mask, part, 0.0) for part in parts for mask in masks])
        left = jnp.concatenate([jnp.concatenate(p, 0) for p in pieces], 1).astype(BF16)
        cut = slice(k * BLK, (k + 1) * BLK)
        term = contract_lanes(left, jnp.concatenate([onehots[end, :, cut] for end in range(2)], 1))
        out = term if out is None else out + term
    n = 8 * high_count
    out = out[0:n] + out[n : 2 * n]
    for k in range(4):
        first = 2 * high_count * k
        own_out[k] = out[first : first + high_count]
        next_out[k] = out[first + high_count : first + 2 * high_count]


def select_kernel(*refs):
    packs, (near_out, centre_out) = refs[:-2], refs[-2:]
    blocks = packs[0].shape[0] // FIELDS
    rows = lax.broadcasted_iota(jnp.int32, (8, BLK), 0)
    for d, ref in enumerate(packs):
        for k in range(blocks):
            w = d * blocks + k
            c = [row(ref, x, k) for x in range(3)]
            centre = LOG2E * rows_at(ref, 0, k)
            extra = choose(rows, {6: LOG2E * dot3(c, c), 7: LOG2E}, 0.0)
            near_out[w] = right_order(split3(jnp.where(rows < 3, -2.0 * centre, extra)))
            parts = split3(jnp.where(rows < 3, centre, choose(rows, {6: -LOG2E}, 0.0)))
            centre_out[w] = jnp.concatenate(parts, 0)


def near_tiles(
    high_count, targets, sources, keep, first_domain, near_s, centre_s, packs, nodes, make_target,
    tgt_s, src_s, acc_s, t_list, w_list,
):
    blocks = packs[0].shape[0] // FIELDS
    base = first_domain * blocks
    rows = lax.broadcasted_iota(jnp.int32, (8, BLK), 0)
    acc_s[...] = jnp.zeros_like(acc_s)
    entries = ((targets[0, k], sources[0, k]) for k in range(targets.shape[1]))
    count = compact(entries, keep, base, blocks, NEAR_GROUP, t_list, w_list)
    zero = jnp.zeros((8, BLK), F32)
    nothing = jnp.zeros((48, BLK), BF16)
    signs = choose(rows, {4: -LOG2E}, zero + LOG2E)
    turn = jnp.where(rows < 3, -2.0, choose(rows, {3: 1.0}, zero))
    constant = split3(choose(rows, {5: LOG2E}, zero))
    for d, ref in enumerate(packs):
        for k in range(blocks):
            w = d * blocks + k
            v = [zero] * 3
            for end in range(2):
                high, low = end_address(nodes[d], 3, end, k, high_count)
                for owner in range(2):
                    for first in range(0, high_count, 8):
                        mask = rows + (owner * high_count + first) == high
                        for x in range(3):
                            table = nodes[d + owner][x, first : first + 8, :]
                            got = jnp.take_along_axis(table, low, axis=1, mode="promise_in_bounds")
                            v[x] = v[x] + jnp.where(mask, got, 0.0)
            for x in range(3):
                for shift in (4, 2, 1):
                    v[x] = v[x] + pltpu.roll(v[x], shift, 0)
                v[x] = v[x] * (0.5 * TIME_STEP)
            c = [row(ref, x, k) for x in range(3)]
            vv, cv = dot3(v, v), dot3(c, v)
            moved = choose(rows, {0: v[0], 1: v[1], 2: v[2], 3: vv}, cv)
            parts = split3(moved * signs)
            centre = centre_s[base + w]
            still = [centre[8 * n : 8 * n + 8] for n in range(3)]
            src_s[w, 0:48, 0:BLK] = right_order([jnp.where(rows < 3, p, 0.0) for p in parts])
            src_s[w, 48:96, 0:BLK] = right_order(
                [jnp.where(rows == 4, p, q) for p, q in zip(parts, still)]
            )
            src_s[w, 0:48, BLK : 2 * BLK] = nothing
            src_s[w, 48:96, BLK : 2 * BLK] = right_order(
                [p * turn + q for p, q in zip(parts, constant)]
            )
            if make_target is not None and d == 0:
                first = choose(rows, {6: 1.0, 7: dot3(c, c)}, rows_at(ref, 0, k))
                second = choose(rows, {3: 1.0, 4: 1.0, 5: vv, 6: cv, 7: 0.0}, moved)
                make_target(k, jnp.concatenate([six_left(first), six_left(second)], 0).T)

    def some_pairs(first, number):
        for u in range(number):
            t = t_list[first + u]
            w = w_list[first + u]
            target = tgt_s[jnp.minimum(t, blocks - 1)]
            rr = jnp.dot(target[:, 0:48], near_s[base + w], preferred_element_type=F32)
            both = jnp.dot(target, src_s[w], preferred_element_type=F32)
            toward = both[:, 0:BLK]
            square = jnp.maximum(both[:, BLK : 2 * BLK], 0.0)
            s = jnp.clip(toward / (square + LOG2E * CORE_SQUARE), 0.0, 1.0)
            acc_s[t] += jnp.exp2(s * (toward + (toward - s * square)) - rr)

    in_groups(count, NEAR_GROUP, some_pairs)


def first_near(high_count, targets, sources, near_s, centre_s, *refs):
    packs, nodes = refs[: REACH + 1], refs[REACH + 1 : 2 * REACH + 3]
    acc_out, tgt_out, vel_out, tgt_s, src_s, t_list, w_list = refs[2 * REACH + 3 :]
    base = REACH * (packs[0].shape[0] // FIELDS)
    for k in range(high_count):
        for x in range(3):
            vel_out[x : x + 1, k * BLK : (k + 1) * BLK] = nodes[0][x, k : k + 1, :]

    def make_target(k, value):
        tgt_out[k] = value
        tgt_s[k] = value.astype(BF16)

    near_tiles(
        high_count, targets, sources, lambda w: w >= base, REACH, near_s, centre_s, packs, nodes,
        make_target, tgt_s, src_s, acc_out, t_list, w_list,
    )


def last_near(high_count, targets, sources, near_s, centre_s, first_acc, tgt, *refs):
    packs, nodes = refs[:REACH], refs[REACH : 2 * REACH + 1]
    near_out, tgt_s, src_s, acc_s, t_list, w_list = refs[2 * REACH + 1 :]
    blocks = tgt.shape[0]
    for t in range(blocks):
        tgt_s[t] = tgt[t].astype(BF16)
    near_tiles(
        high_count, targets, sources, lambda w: w < REACH * blocks, 0, near_s, centre_s, packs, nodes,
        None, tgt_s, src_s, acc_s, t_list, w_list,
    )
    for t in range(blocks):
        near_out[t : t + 1] = jnp.sum((first_acc[t] + acc_s[t]).T, axis=0, keepdims=True)


def velocity_kernel(mobility, numbers, *refs):
    out = refs[-1]
    total = refs[0][...]
    for ref in refs[1:-1]:
        total = total + ref[...]
    scale = mobility[...] / (1.0 + total[3])
    for x in range(3):
        out[x] = total[x] * scale
    out[3:7] = numbers[...]


def rows_of(pieces, first, rows):
    total = None
    for piece in pieces:
        last = first + piece.shape[0]
        padded = jnp.pad(piece, ((first, rows - last), (0, 0)))
        total = padded if total is None else total + padded
        first = last
    return total


def local(
    centres, seg_lines, burgers, neighbour_blocks, seg_nodes, node_owner, mobility, cand_target, cand_source
):
    seg = centres.shape[1]
    blocks = seg // BLK
    high_count = mobility.shape[0] // BLK
    lanes = lax.axis_size("lanes")
    window = (2 * REACH + 1) * blocks
    fields = rows_of([centres, burgers, seg_lines], 0, FIELDS + 4)
    fields = fields + rows_of([seg_nodes, node_owner], FIELDS, FIELDS + 4).astype(F32)
    own, numbers = pl.pallas_call(
        pack_kernel,
        out_shape=(
            jax.ShapeDtypeStruct((FIELDS * blocks, BLK), F32),
            jax.ShapeDtypeStruct((4, blocks, BLK), F32),
        ),
        in_specs=[VM],
        out_specs=(VM, VM),
        compiler_params=params(4),
        name="pack",
    )(fields)
    packs = [own if o == 0 else shifted(own, o) for o in range(-REACH, REACH + 1)]
    small = [
        neighbour_blocks,
        mobility.reshape(high_count, BLK),
        cand_target.reshape(1, -1),
        cand_source.reshape(1, -1),
    ]
    lists, rate, targets, sources, lhs, own_onehots = pl.pallas_call(
        functools.partial(early_kernel, high_count),
        out_shape=[jax.ShapeDtypeStruct(x.shape, x.dtype) for x in small]
        + [
            jax.ShapeDtypeStruct((blocks, BLK, 48), F32),
            jax.ShapeDtypeStruct((2, BLK, seg), BF16),
        ],
        in_specs=[VM] * (2 + len(small)),
        out_specs=[VM] * (2 + len(small)),
        compiler_params=params(8),
        cost_estimate=long_call(),
        name="early",
    )(own, numbers, *small)

    entry_room = pltpu.SMEM((lists.shape[0] * lists.shape[1] + FORCE_GROUP,), jnp.int32)
    accumulator = (blocks + 1, BLK, 32)

    def force_scratch(domains):
        return [
            pltpu.VMEM((blocks, BLK, 48), BF16),
            pltpu.VMEM((domains * blocks, 48, 2 * BLK), BF16),
            pltpu.VMEM((domains * blocks, 32, BLK), BF16),
        ]

    first_acc = pl.pallas_call(
        first_forces,
        out_shape=jax.ShapeDtypeStruct(accumulator, F32),
        in_specs=[SM] + [VM] * (2 + REACH),
        out_specs=VM,
        scratch_shapes=force_scratch(REACH + 1) + [entry_room] * 2,
        compiler_params=params(16),
        cost_estimate=long_call(),
        name="first_forces",
    )(lists, lhs, *packs[REACH:])
    part = jax.ShapeDtypeStruct((4, high_count, BLK), F32)
    own_part, next_part = pl.pallas_call(
        functools.partial(last_forces, lanes, high_count),
        out_shape=(part, part),
        in_specs=[SM] + [VM] * (5 + REACH),
        out_specs=(VM, VM),
        scratch_shapes=force_scratch(REACH)
        + [pltpu.VMEM(accumulator, F32), pltpu.VMEM((blocks, 8, BLK), F32)]
        + [entry_room] * 2,
        compiler_params=params(16),
        name="last_forces",
    )(lists, lhs, own_onehots, numbers, own, first_acc, *packs[:REACH])
    terms = [own_part]
    terms += [shifted(own_part, 0, lane) for lane in range(1, lanes)]
    terms += [shifted(next_part, -1, lane) for lane in range(lanes)]
    velocity = pl.pallas_call(
        velocity_kernel,
        out_shape=jax.ShapeDtypeStruct((7, high_count, BLK), F32),
        in_specs=[VM] * (2 + len(terms)),
        out_specs=VM,
        compiler_params=params(4),
        name="velocity",
    )(rate, numbers, *terms)
    nodes = [velocity if o == 0 else shifted(velocity, o) for o in range(-REACH, REACH + 2)]
    near_sources, centre_sources = pl.pallas_call(
        select_kernel,
        out_shape=(
            jax.ShapeDtypeStruct((window, 48, BLK), BF16),
            jax.ShapeDtypeStruct((window, 24, BLK), F32),
        ),
        in_specs=[VM] * len(packs),
        out_specs=(VM, VM),
        compiler_params=params(16),
        cost_estimate=long_call(),
        name="select",
    )(*packs)

    pair_room = pltpu.SMEM((targets.shape[1] + NEAR_GROUP,), jnp.int32)
    accumulator = (blocks + 1, BLK, BLK)

    def near_scratch(domains):
        return [
            pltpu.VMEM((blocks, BLK, 96), BF16),
            pltpu.VMEM((domains * blocks, 96, 2 * BLK), BF16),
        ]

    first_sum, target_rows, vel = pl.pallas_call(
        functools.partial(first_near, high_count),
        out_shape=(
            jax.ShapeDtypeStruct(accumulator, F32),
            jax.ShapeDtypeStruct((blocks, BLK, 96), F32),
            jax.ShapeDtypeStruct((3, high_count * BLK), F32),
        ),
        in_specs=[SM, SM] + [VM] * (5 + 2 * REACH),
        out_specs=(VM, VM, VM),
        scratch_shapes=near_scratch(REACH + 1) + [pair_room] * 2,
        compiler_params=params(16),
        cost_estimate=long_call(),
        name="first_near",
    )(targets, sources, near_sources, centre_sources, *packs[REACH:], *nodes[REACH:])
    near = pl.pallas_call(
        functools.partial(last_near, high_count),
        out_shape=jax.ShapeDtypeStruct((blocks, BLK), F32),
        in_specs=[SM, SM] + [VM] * (5 + 2 * REACH),
        out_specs=VM,
        scratch_shapes=near_scratch(REACH) + [pltpu.VMEM(accumulator, F32)] + [pair_room] * 2,
        compiler_params=params(16),
        name="last_near",
    )(
        targets, sources, near_sources, centre_sources, first_sum, target_rows,
        *packs[:REACH], *nodes[: REACH + 1],
    )
    return vel, near.reshape(seg)


def solution(mesh):
    in_specs = (
        P(None, "cells"),
        P(None, "cells"),
        P(None, "cells"),
        P("cells", "lanes"),
        P(None, "cells"),
        P(None, "cells"),
        P("cells"),
        P("cells"),
        P("cells"),
    )
    out_specs = (P(None, "cells"), P("cells"))

    return jax.shard_map(local, mesh=mesh, in_specs=in_specs, out_specs=out_specs, check_vma=False)
```
